128 devices in a mesh: vec: 16 (over y, x_lo, core), cent: 8 (over x_hi, z).
Axes of the slice: x: 4 (x_hi: 2, x_lo: 2; x = x_hi * 2 + x_lo), y: 4, z: 4, core: 2. Of those that a mesh axis runs over, the one named last changes fastest.
Arguments:
- weights: bfloat16 [32768, 256], P('vec'), may hold values from -44 to 44
- centroids: bfloat16 [8192, 256], P('cent'), may hold values from -4 to 4
- cotangent: bfloat16 [32768, 256], P('vec'), may hold values from -6 to 6
Outputs:
- grad_weights: bfloat16 [32768, 256], P('vec')
- grad_centroids: float32 [8192, 256], P('cent')
The draws below stay inside these ranges and needn't reach their ends.
All inputs are finite; a program needn't handle non-finite values.
Results may differ from the reference program's by a relative error of at most 0.02.
The reference program's roundings to bfloat16 on the way count: a program that leaves them out, or rounds other values in their place, can miss the bound.
Values may be sent and summed in bfloat16 or wider, within the bound.
A program may use at most 128 MiB of HBM per device.

```python
import jax
import jax.numpy as jnp
from jax import lax

D = 256
K = 8192
V_DEV = 2048
VECTORS = 32768


def draw_pair(key):
    keys = jax.random.split(jax.random.fold_in(key, 7), 2)
    cent = jnp.clip(jax.random.normal(keys[0], (K, D), jnp.float32), -4.0, 4.0)
    vecs = jnp.clip(jax.random.normal(keys[1], (VECTORS, D), jnp.float32), -4.0, 4.0)
    return (vecs, cent)


def draw_weights(key, part):
    vecs, cent = draw_pair(key)
    return vecs.astype(jnp.bfloat16)


def draw_centroids(key, part):
    vecs, cent = draw_pair(key)
    return cent.astype(jnp.bfloat16)


def steps_of(stream_key, shape, shards, smallest, high):
    def one(position, shards_of):
        steps = jax.random.uniform(jax.random.fold_in(jax.random.fold_in(stream_key, 6), position), (shards_of,), jnp.float32, smallest / len(shards), high / len(shards))
        return jnp.repeat(jnp.exp(steps), shape[position] // shards_of).reshape((-1,) + (1,) * (len(shape) - position - 1))

    gain = one(*shards[0])
    for cut in shards[1:]:
        gain = gain * one(*cut)
    return gain


def scatter_about(rng, dims, scale, limit, shards=(), dtype=jnp.bfloat16):
    values = scale * jax.random.normal(rng, dims, jnp.float32)
    if shards:
        values = values * steps_of(rng, dims, shards, -0.22, 0.18)
    return jnp.clip(values, -limit, limit).astype(dtype)


def setup_inputs(seed: int = 0) -> dict:
    key_list = jax.random.split(jax.random.key(seed), 4)
    return {
        "weights": draw_weights(jax.random.fold_in(key_list[3], 71), 0),
        "centroids": draw_centroids(jax.random.fold_in(key_list[3], 71), 0),
        "cotangent": scatter_about(key_list[2], (VECTORS, D), 1.0, 6.0, ((0, 16),)),
    }


def logits(rows, cent):
    cross = jnp.dot(rows, cent.T, preferred_element_type=jnp.float32)
    square = jnp.sum(jnp.square(cent.astype(jnp.float32)), axis=1)
    return (2.0 * cross - square[None, :]) * (D ** -0.5)


def soften(score):
    top = jnp.max(score, axis=1, keepdims=True)
    expo = jnp.exp(score - top)
    return expo / jnp.sum(expo, axis=1, keepdims=True)


def reference(weights, centroids, cotangent):
    blocks = weights.shape[0] // V_DEV
    wblock = weights.reshape(blocks, V_DEV, D)
    gblock = cotangent.reshape(blocks, V_DEV, D)
    scale = 2.0 * D ** -0.5

    def first_pass(carry, rows):
        mass, count = carry
        resp = soften(logits(rows, centroids))
        mass = mass + jnp.dot(resp.astype(jnp.bfloat16).T, rows, preferred_element_type=jnp.float32)
        count = count + jnp.sum(resp, axis=0)
        return (mass, count), None

    init = (jnp.zeros((K, D), jnp.float32), jnp.zeros((K,), jnp.float32))
    (mass, count), _ = lax.scan(first_pass, init, wblock)
    denom = count + 1e-6
    moved = (mass / denom[:, None]).astype(jnp.bfloat16)
    moved_f = moved.astype(jnp.float32)

    def second_pass(carry, pair):
        rows, cot = pair
        resp = soften(logits(rows, moved))
        dresp = jnp.dot(cot, moved.T, preferred_element_type=jnp.float32)
        dots = jnp.sum(resp * dresp, axis=1, keepdims=True)
        edge = resp * (dresp - dots) * scale
        edge_b = edge.astype(jnp.bfloat16)
        part = jnp.dot(edge_b, moved, preferred_element_type=jnp.float32)
        carry = carry + jnp.dot(resp.astype(jnp.bfloat16).T, cot, preferred_element_type=jnp.float32)
        carry = carry + jnp.dot(edge_b.T, rows, preferred_element_type=jnp.float32)
        carry = carry - jnp.sum(edge, axis=0)[:, None] * moved_f
        return carry, part

    moved_cot, part_two = lax.scan(second_pass, jnp.zeros((K, D), jnp.float32), (wblock, gblock))
    mean_cot = (moved_cot / denom[:, None]).astype(jnp.bfloat16)
    count_cot = -jnp.sum(mean_cot.astype(jnp.float32) * moved_f, axis=1)
    cent_f = centroids.astype(jnp.float32)

    def third_pass(carry, pair):
        rows, part = pair
        resp = soften(logits(rows, centroids))
        dresp = jnp.dot(rows, mean_cot.T, preferred_element_type=jnp.float32) + count_cot[None, :]
        dots = jnp.sum(resp * dresp, axis=1, keepdims=True)
        edge = resp * (dresp - dots) * scale
        edge_b = edge.astype(jnp.bfloat16)
        total = part + jnp.dot(resp.astype(jnp.bfloat16), mean_cot, preferred_element_type=jnp.float32)
        total = total + jnp.dot(edge_b, centroids, preferred_element_type=jnp.float32)
        carry = carry + jnp.dot(edge_b.T, rows, preferred_element_type=jnp.float32)
        carry = carry - jnp.sum(edge, axis=0)[:, None] * cent_f
        return carry, total.astype(jnp.bfloat16)

    start_cot, grad_rows = lax.scan(third_pass, jnp.zeros((K, D), jnp.float32), (wblock, part_two))
    return grad_rows.reshape(blocks * V_DEV, D), start_cot
```

```python
import functools
import math

import jax
import jax.numpy as jnp
from jax import lax
from jax.experimental import pallas as pl
from jax.experimental.pallas import tpu as pltpu
from jax.sharding import PartitionSpec as P

MESH = pl.DeviceIdType.MESH
F32 = jnp.float32
BF16 = jnp.bfloat16
CHUNKS = 4
LANES = 128
LOG2E = math.log2(math.e)


def dot_nn(a, b):
    return lax.dot_general(a, b, (((1,), (0,)), ((), ())), preferred_element_type=F32)


def dot_nt(a, b):
    return lax.dot_general(a, b, (((1,), (1,)), ((), ())), preferred_element_type=F32)


def folded(x):
    return jnp.sum(x.reshape(x.shape[0] // 8, 8, x.shape[1]), axis=0)


def peaked(x):
    return jnp.max(x.reshape(x.shape[0] // 8, 8, x.shape[1]), axis=0)


def lane_folded(x):
    parts = [x[:, at : at + LANES] for at in range(0, x.shape[1], LANES)]
    return functools.reduce(jnp.add, parts)


def wide(column, width):
    return jnp.concatenate([column] * (width // LANES), axis=1)


def kernel(
    peers, groups, w, c, g, gw, gc,
    e1, e2, ds, r1b, r2b, eb, sb, ct, mt, moved, mean, part, esum, column, den,
    stat_out, stat_in, row1, row2, cnt_out, cnt_in, mass_out, mass_in, mcot_out, mcot_in,
    start_out, start_in, own_moved, own_mean, own_start, start_all, grad_out, grad_in, own_grad,
    start_f, stat_send, stat_recv, send, recv, local,
):
    vectors, depth = w.shape
    cents = c.shape[0]
    block = vectors // groups
    share = cents // peers
    rows_of = cents // CHUNKS
    owners = peers // CHUNKS
    step = min(64, rows_of)
    vec = lax.axis_index("vec")
    cent = lax.axis_index("cent")
    scale = 2.0 * depth ** (-0.5)
    slope = 2.0 * depth ** (-0.5) * LOG2E
    offset = depth ** (-0.5) * LOG2E

    def along(axis, distance):
        if axis == "vec":
            return {"vec": lax.rem(vec + distance, peers)}
        return {"cent": lax.rem(cent + distance, groups)}

    def start(src, dst, sems, device):
        pltpu.make_async_remote_copy(
            src_ref=src, dst_ref=dst, send_sem=sems[0], recv_sem=sems[1],
            device_id=device, device_id_type=MESH,
        ).start()

    def wait_recv(ref, sem):
        pltpu.make_async_copy(ref, ref, sem).wait()

    def cols_of(j):
        return pl.ds(pl.multiple_of(j * block, block), block)

    def chunk_of(t):
        return lax.rem(vec // owners + t, CHUNKS)

    def rows_at(r):
        return pl.ds(pl.multiple_of(r * rows_of, rows_of), rows_of)

    barrier = pltpu.get_barrier_semaphore()
    for far in range(1, peers):
        pl.semaphore_signal(barrier, inc=1, device_id=along("vec", far), device_id_type=MESH)
    for far in range(1, groups):
        pl.semaphore_signal(barrier, inc=1, device_id=along("cent", far), device_id_type=MESH)

    def squares(ref):
        for at in range(0, cents, step):
            f = ref[at : at + step, :].astype(F32)
            total = jnp.sum(f * f, axis=1, keepdims=True) * offset
            sb[at : at + step, :] = jnp.broadcast_to(total, (step, block))

    def soften_block(cols, scores, cot):
        top = None
        for at in range(0, cents, step):
            here = peaked(scores[at : at + step, cols])
            top = here if top is None else jnp.maximum(top, here)
        top = jnp.max(top, axis=0, keepdims=True)
        total = dots = 0.0
        for at in range(0, cents, step):
            expo = jnp.exp2(scores[at : at + step, cols] - top)
            scores[at : at + step, cols] = expo
            total = total + folded(expo)
            if cot is not None:
                dots = dots + folded(expo * cot[at : at + step, cols])
        total = jnp.sum(total, axis=0, keepdims=True)
        if cot is None:
            return top, total, None
        return top, total, jnp.sum(dots, axis=0, keepdims=True)

    def send_stats(which, j, lines):
        for far in range(1, groups):
            start(
                stat_out.at[which, j, 0:lines],
                stat_in.at[which, j, groups - far, 0:lines],
                (stat_send, stat_recv.at[which, j]),
                along("cent", far),
            )

    def wait_stats(which, j, lines):
        ref = stat_in.at[which, j, 1:groups, 0:lines]
        wait_recv(ref, stat_recv.at[which, j])

    squares(c)
    pl.semaphore_wait(barrier, peers + groups - 2)

    def first_block(j, carry):
        cols = cols_of(j)
        cross = dot_nt(c[...], w[cols, :])
        for at in range(0, cents, step):
            e1[at : at + step, cols] = cross[at : at + step] * slope - sb[at : at + step, :]
        top, total, _ = soften_block(cols, e1, None)
        stat_out[0, j, 0:1, :] = top
        stat_out[0, j, 1:2, :] = total
        stat_in[0, j, 0, 0:1, :] = top
        stat_in[0, j, 0, 1:2, :] = total
        send_stats(0, j, 8)
        return carry

    lax.fori_loop(0, groups, first_block, 0)
    ct[...] = c[...].astype(F32).T.astype(BF16)

    def combine(which, j):
        peak = stat_in[which, j, 0, 0:1, :]
        for q in range(1, groups):
            peak = jnp.maximum(peak, stat_in[which, j, q, 0:1, :])
        total = dots = 0.0
        for q in range(groups):
            part_of = jnp.exp2(stat_in[which, j, q, 0:1, :] - peak)
            total = total + part_of * stat_in[which, j, q, 1:2, :]
            if which:
                dots = dots + part_of * stat_in[which, j, q, 2:3, :]
        mine = jnp.exp2(stat_in[which, j, 0, 0:1, :] - peak)
        return mine / total, dots / total

    def first_factor(j, carry):
        wait_stats(0, j, 8)
        row1[j, 0:1, :] = combine(0, j)[0]
        return carry

    lax.fori_loop(0, groups, first_factor, 0)

    def to_owners(r, which, out, arrived, extra=None):
        def one(q, carry):
            owner = r * owners + q
            far = lax.rem(owner - vec + peers, peers)
            slot = lax.rem(peers - far, peers)

            @pl.when(far != 0)
            def _():
                sems = (send.at[which], recv.at[which])
                start(out.at[owner], arrived.at[slot], sems, {"vec": owner})
                if extra is not None:
                    sems = (send.at[which + 1], recv.at[which + 1])
                    start(extra[0].at[r], extra[1].at[slot], sems, {"vec": owner})

            @pl.when(far == 0)
            def _():
                arrived[0] = out[owner]
                if extra is not None:
                    extra[1][0] = extra[0][r]

            return carry

        lax.fori_loop(0, owners, one, 0)

    def mass_chunk(t, carry):
        r = chunk_of(t)
        rows = rows_at(r)
        base = r * rows_of
        for at in range(0, rows_of, step):
            here = pl.ds(pl.multiple_of(base + at, step), step)
            count = 0.0
            for j in range(groups):
                cols = slice(j * block, (j + 1) * block)
                resp = e1[here, cols] * row1[j, 0:1, :]
                r1b[here, cols] = resp.astype(BF16)
                count = count + lane_folded(resp)
            count = jnp.sum(count, axis=1, keepdims=True)
            column[at : at + step, :] = jnp.broadcast_to(count, (step, LANES))
        cnt_out[r] = column[0:rows_of, :].T[0:1, :]
        mass = dot_nn(r1b[rows, :], w[...]).astype(BF16)
        for q in range(owners):
            mass_out[r * owners + q] = mass[q * share : (q + 1) * share]
        to_owners(r, 0, mass_out, mass_in, (cnt_out, cnt_in))
        return carry

    lax.fori_loop(0, CHUNKS, mass_chunk, 0)

    def wait_owners(which, arrived):
        wait_recv(arrived.at[1:peers], recv.at[which])

    def summed(arrived, count):
        total = arrived[0].astype(F32)
        for q in range(1, count):
            total = total + arrived[q].astype(F32)
        return total

    def to_all(which, own, everywhere):
        at = pl.ds(pl.multiple_of(vec * share, share), share)
        for far in range(1, peers):
            sems = (send.at[which], recv.at[which])
            start(own, everywhere.at[at, :], sems, along("vec", far))
        everywhere[at, :] = own[...]

    def wait_all(which, everywhere):
        wait_recv(everywhere.at[0 : (peers - 1) * share, :], recv.at[which])

    wait_owners(1, cnt_in)
    count = cnt_in[0]
    for q in range(1, peers):
        count = count + cnt_in[q]
    column[0:rows_of, :] = jnp.broadcast_to(count, (LANES, rows_of)).T
    mine = pl.ds(pl.multiple_of(lax.rem(vec, owners) * share, share), share)
    den[...] = column[mine, :] + 1e-6
    wait_owners(0, mass_in)
    own_moved[...] = (summed(mass_in, peers) / wide(den[...], depth)).astype(BF16)
    to_all(2, own_moved, moved)
    wait_all(2, moved)

    squares(moved)

    def second_block(j, carry):
        cols = cols_of(j)
        cross = dot_nt(moved[...], w[cols, :])
        for at in range(0, cents, step):
            e2[at : at + step, cols] = cross[at : at + step] * slope - sb[at : at + step, :]
        ds[:, cols] = dot_nt(moved[...], g[cols, :])
        top, total, dots = soften_block(cols, e2, ds)
        for line, value in enumerate((top, total, dots)):
            stat_out[1, j, line : line + 1, :] = value
            stat_in[1, j, 0, line : line + 1, :] = value
        send_stats(1, j, 8)
        return carry

    lax.fori_loop(0, groups, second_block, 0)
    mt[...] = moved[...].astype(F32).T.astype(BF16)

    def second_factor(j, carry):
        wait_stats(1, j, 8)
        factor, dots = combine(1, j)
        row2[j, 0:1, :] = factor
        row2[j, 1:2, :] = dots
        return carry

    lax.fori_loop(0, groups, second_factor, 0)

    def cot_chunk(t, carry):
        r = chunk_of(t)
        rows = rows_at(r)
        base = r * rows_of
        for at in range(0, rows_of, step):
            here = pl.ds(pl.multiple_of(base + at, step), step)
            total = 0.0
            for j in range(groups):
                cols = slice(j * block, (j + 1) * block)
                second = e2[here, cols] * row2[j, 0:1, :]
                r2b[here, cols] = second.astype(BF16)
                edge = second * (ds[here, cols] - row2[j, 1:2, :]) * scale
                eb[here, cols] = edge.astype(BF16)
                total = total + lane_folded(edge)
            total = jnp.sum(total, axis=1, keepdims=True)
            column[at : at + step, :] = jnp.broadcast_to(total, (step, LANES))
        cot = dot_nn(r2b[rows, :], g[...]) + dot_nn(eb[rows, :], w[...])
        for q in range(owners):
            inner = slice(q * share, (q + 1) * share)
            far = pl.ds(pl.multiple_of(base + q * share, share), share)
            value = cot[inner] - wide(column[inner, :], depth) * moved[far, :].astype(F32)
            mcot_out[r * owners + q] = value.astype(BF16)
        to_owners(r, 3, mcot_out, mcot_in)
        return carry

    lax.fori_loop(0, CHUNKS, cot_chunk, 0)

    def part_block(j, carry):
        cols = cols_of(j)
        part[:, cols] = dot_nn(mt[...], eb[:, cols])
        return carry

    lax.fori_loop(0, groups, part_block, 0)

    wait_owners(3, mcot_in)
    own_mean[...] = (summed(mcot_in, peers) / wide(den[...], depth)).astype(BF16)
    to_all(4, own_mean, mean)
    wait_all(4, mean)

    for at in range(0, cents, step):
        here = slice(at, at + step)
        total = jnp.sum(mean[here, :].astype(F32) * moved[here, :].astype(F32), axis=1, keepdims=True)
        sb[here, :] = jnp.broadcast_to(total, (step, block))

    def third_block(t, carry):
        j = lax.rem(cent + 1 + t, groups)
        cols = cols_of(j)
        cross = dot_nt(mean[...], w[cols, :])
        dots = 0.0
        for at in range(0, cents, step):
            dfirst = cross[at : at + step] - sb[at : at + step, :]
            ds[at : at + step, cols] = dfirst
            dots = dots + folded(e1[at : at + step, cols] * dfirst)
        dots = jnp.sum(dots, axis=0, keepdims=True) * row1[j, 0:1, :]
        stat_out[2, j, 0:1, :] = dots
        stat_in[2, j, 0, 0:1, :] = dots
        send_stats(2, j, 8)
        return carry

    lax.fori_loop(0, groups, third_block, 0)
    mt[...] = mean[...].astype(F32).T.astype(BF16)

    def grad_block(t, carry):
        j = lax.rem(cent + 1 + t, groups)
        cols = cols_of(j)
        wait_stats(2, j, 8)
        dots = stat_in[2, j, 0, 0:1, :]
        for q in range(1, groups):
            dots = dots + stat_in[2, j, q, 0:1, :]
        factor = row1[j, 0:1, :]
        for at in range(0, cents, step):
            first = e1[at : at + step, cols] * factor
            edge = first * (ds[at : at + step, cols] - dots) * scale
            eb[at : at + step, cols] = edge.astype(BF16)
            total = lane_folded(edge)

            @pl.when(t == 0)
            def _():
                esum[at : at + step, :] = total

            @pl.when(t != 0)
            def _():
                esum[at : at + step, :] += total

        grad = part[:, cols] + dot_nn(mt[...], r1b[:, cols]) + dot_nn(ct[...], eb[:, cols])
        grad_out[j] = grad.astype(BF16)

        @pl.when(t != groups - 1)
        def _():
            slot = lax.rem(cent - j + groups, groups)
            start(grad_out.at[j], grad_in.at[slot], (send.at[5], recv.at[5]), {"cent": j})

        @pl.when(t == groups - 1)
        def _():
            grad_in[0] = grad_out[j]

        return carry

    lax.fori_loop(0, groups, grad_block, 0)

    def start_chunk(t, carry):
        r = chunk_of(t)
        rows = rows_at(r)
        base = r * rows_of
        cot = dot_nn(eb[rows, :], w[...])
        for q in range(owners):
            inner = slice(q * share, (q + 1) * share)
            far = pl.ds(pl.multiple_of(base + q * share, share), share)
            total = jnp.sum(esum[far, :], axis=1, keepdims=True)
            value = cot[inner] - total * c[far, :].astype(F32)
            start_out[r * owners + q] = value.astype(BF16)
        to_owners(r, 6, start_out, start_in)
        return carry

    lax.fori_loop(0, CHUNKS, start_chunk, 0)

    wait_recv(grad_in.at[1:groups], recv.at[5])
    own_grad[...] = summed(grad_in, groups).T.astype(BF16)
    mine = pl.ds(pl.multiple_of(cent * block, block), block)
    for far in range(1, groups):
        start(own_grad, gw.at[mine, :], (send.at[7], recv.at[7]), along("cent", far))
    keep = pltpu.make_async_copy(own_grad, gw.at[mine, :], local.at[0])
    keep.start()

    wait_owners(6, start_in)
    own_start[...] = summed(start_in, peers).astype(BF16)
    to_all(8, own_start, start_all)
    wait_all(8, start_all)
    start_f[...] = start_all[...].astype(F32)
    result = pltpu.make_async_copy(start_f, gc, local.at[1])
    result.start()
    wait_recv(gw.at[0 : (groups - 1) * block, :], recv.at[7])
    keep.wait()
    result.wait()

    wait_recv(stat_in.at[:, :, 1:groups], stat_send)
    wait_recv(mass_in.at[1:peers], send.at[0])
    wait_recv(cnt_in.at[1:peers], send.at[1])
    wait_recv(mcot_in.at[1:peers], send.at[3])
    wait_recv(start_in.at[1:peers], send.at[6])
    wait_recv(grad_in.at[1:groups], send.at[5])
    wait_recv(gw.at[0 : (groups - 1) * block, :], send.at[7])
    for which, ref in ((2, moved), (4, mean), (8, start_all)):
        wait_recv(ref.at[0 : (peers - 1) * share, :], send.at[which])


def body(peers, groups, weights, centroids, cotangent):
    vectors, depth = weights.shape
    cents = centroids.shape[0]
    block = vectors // groups
    share = cents // peers
    rows_of = cents // CHUNKS
    vmem = pltpu.VMEM
    scratch = [
        vmem((cents, vectors), F32),
        vmem((cents, vectors), F32),
        vmem((cents, vectors), F32),
        vmem((cents, vectors), BF16),
        vmem((cents, vectors), BF16),
        vmem((cents, vectors), BF16),
        vmem((cents, block), F32),
        vmem((depth, cents), BF16),
        vmem((depth, cents), BF16),
        vmem((cents, depth), BF16),
        vmem((cents, depth), BF16),
        vmem((depth, vectors), F32),
        vmem((cents, LANES), F32),
        vmem((rows_of, LANES), F32),
        vmem((share, LANES), F32),
        vmem((3, groups, 8, block), F32),
        vmem((3, groups, groups, 8, block), F32),
        vmem((groups, 8, block), F32),
        vmem((groups, 8, block), F32),
        vmem((CHUNKS, 1, rows_of), F32),
        vmem((peers, 1, rows_of), F32),
        vmem((peers, share, depth), BF16),
        vmem((peers, share, depth), BF16),
        vmem((peers, share, depth), BF16),
        vmem((peers, share, depth), BF16),
        vmem((peers, share, depth), BF16),
        vmem((peers, share, depth), BF16),
        vmem((share, depth), BF16),
        vmem((share, depth), BF16),
        vmem((share, depth), BF16),
        vmem((cents, depth), BF16),
        vmem((groups, depth, block), BF16),
        vmem((groups, depth, block), BF16),
        vmem((block, depth), BF16),
        vmem((cents, depth), F32),
        pltpu.SemaphoreType.DMA,
        pltpu.SemaphoreType.DMA((3, groups)),
        pltpu.SemaphoreType.DMA((9,)),
        pltpu.SemaphoreType.DMA((9,)),
        pltpu.SemaphoreType.DMA((2,)),
    ]
    return pl.pallas_call(
        functools.partial(kernel, peers, groups),
        out_shape=(
            jax.ShapeDtypeStruct((vectors, depth), BF16),
            jax.ShapeDtypeStruct((cents, depth), F32),
        ),
        in_specs=[pl.BlockSpec(memory_space=pltpu.VMEM)] * 3,
        out_specs=[pl.BlockSpec(memory_space=pl.ANY)] * 2,
        scratch_shapes=scratch,
        compiler_params=pltpu.CompilerParams(
            collective_id=0, has_side_effects=True, vmem_limit_bytes=67043328
        ),
        name="soft_assignments",
    )(weights, centroids, cotangent)


def solution(mesh):
    return jax.shard_map(
        functools.partial(body, mesh.shape["vec"], mesh.shape["cent"]),
        mesh=mesh,
        in_specs=(P("vec", None), P("cent", None), P("vec", None)),
        out_specs=(P("vec", None), P("cent", None)),
        check_vma=False,
    )
```

```python
import functools
import math

import jax
import jax.numpy as jnp
from jax import lax
from jax.experimental import pallas as pl
from jax.experimental.pallas import tpu as pltpu
from jax.sharding import PartitionSpec as P

MESH = pl.DeviceIdType.MESH
F32 = jnp.float32
BF16 = jnp.bfloat16
CORES = 2
PAIR = 2
STATS = (2, 3, 1)
LANES = 128
LOG2E = math.log2(math.e)


def dot_nn(a, b):
    return lax.dot_general(a, b, (((1,), (0,)), ((), ())), preferred_element_type=F32)


def dot_nt(a, b):
    return lax.dot_general(a, b, (((1,), (1,)), ((), ())), preferred_element_type=F32)


def folded(x):
    return jnp.sum(x.reshape(x.shape[0] // 8, 8, x.shape[1]), axis=0)


def peaked(x):
    return jnp.max(x.reshape(x.shape[0] // 8, 8, x.shape[1]), axis=0)


def lane_folded(x):
    parts = [x[:, at : at + LANES] for at in range(0, x.shape[1], LANES)]
    return functools.reduce(jnp.add, parts)


def wide(column, width):
    return jnp.concatenate([column] * (width // LANES), axis=1)


def kernel(
    peers, groups, w, c, g, gw, gc,
    e1, e2, ds, r1b, r2b, eb, sb, ct, mt, moved, mean, part, esum, column, den,
    stat_out, stat_in, row1, row2, cnt_out, cnt_near, cnt_both, cnt_in, near_out, near_in, sum_out, sum_in,
    own_moved, own_mean, own_start, start_all, grad_out, grad_in, pair_keep, pair_out, pair_in, own_grad,
    stat_send, stat_recv, near_send, near_recv, cnt_send, cnt_recv, sum_send, sum_recv, all_send, all_recv,
    both_send, both_recv, grad_send, grad_recv, pair_send, pair_recv, out_send, out_recv, local,
):
    vectors, depth = w.shape
    cents = c.shape[0]
    block = vectors // groups
    half = vectors // 2
    piece = half // groups
    share = cents // peers
    chips = peers // CORES
    ring_y = chips // PAIR
    ring_z = groups // PAIR
    rows_of = cents // ring_y
    owners = PAIR * CORES
    step = min(64, rows_of)
    vec = lax.axis_index("vec")
    cent = lax.axis_index("cent")
    chip, core = vec // CORES, lax.rem(vec, CORES)
    y, x_low = chip // PAIR, lax.rem(chip, PAIR)
    x_high, z = cent // ring_z, lax.rem(cent, ring_z)
    sibling = {"vec": vec + 1 - 2 * core}
    scale = 2.0 * depth ** (-0.5)
    slope = 2.0 * depth ** (-0.5) * LOG2E
    offset = depth ** (-0.5) * LOG2E

    def start(src, dst, send, recv, device):
        pltpu.make_async_remote_copy(
            src_ref=src, dst_ref=dst, send_sem=send, recv_sem=recv,
            device_id=device, device_id_type=MESH,
        ).start()

    def wait(ref, sem):
        pltpu.make_async_copy(ref, ref, sem).wait()

    def cent_at(far):
        return {"cent": lax.rem(cent + far, groups)}

    def chip_at(far):
        return lax.rem(chip + far, chips)

    def cols_of(j):
        return pl.ds(pl.multiple_of(j * block, block), block)

    def chunk_of(t):
        return lax.rem(y + 1 + t, ring_y)

    def rows_at(r):
        return pl.ds(pl.multiple_of(r * rows_of, rows_of), rows_of)

    def rows_from(owner):
        return pl.ds(pl.multiple_of(owner * share, share), share)

    barrier = pltpu.get_barrier_semaphore()
    pl.semaphore_signal(barrier, inc=1, device_id=sibling, device_id_type=MESH)
    for far in range(1, chips):
        there = {"vec": chip_at(far) * CORES + core}
        pl.semaphore_signal(barrier, inc=1, device_id=there, device_id_type=MESH)
    for far in range(1, groups):
        pl.semaphore_signal(barrier, inc=1, device_id=cent_at(far), device_id_type=MESH)

    def squares(ref):
        for at in range(0, cents, step):
            f = ref[at : at + step, :].astype(F32)
            total = jnp.sum(f * f, axis=1, keepdims=True) * offset
            sb[at : at + step, :] = jnp.broadcast_to(total, (step, block))

    def soften_block(cols, scores, cot):
        top = None
        for at in range(0, cents, step):
            here = peaked(scores[at : at + step, cols])
            top = here if top is None else jnp.maximum(top, here)
        top = jnp.max(top, axis=0, keepdims=True)
        total = dots = 0.0
        for at in range(0, cents, step):
            expo = jnp.exp2(scores[at : at + step, cols] - top)
            scores[at : at + step, cols] = expo
            total = total + folded(expo)
            if cot is not None:
                dots = dots + folded(expo * cot[at : at + step, cols])
        total = jnp.sum(total, axis=0, keepdims=True)
        if cot is None:
            return top, total
        return top, total, jnp.sum(dots, axis=0, keepdims=True)

    def send_stats(which, j, values):
        lanes = slice(0, len(values) * block)
        for line, value in enumerate(values):
            inner = slice(line * block, (line + 1) * block)
            stat_out[which, j, :, inner] = value
            stat_in[which, j, 0, :, inner] = value
        for far in range(1, groups):
            start(
                stat_out.at[which, j, :, lanes],
                stat_in.at[which, j, groups - far, :, lanes],
                stat_send.at[which],
                stat_recv.at[which, j],
                cent_at(far),
            )

    def wait_stats(which, j):
        lanes = slice(0, STATS[which] * block)
        wait(stat_in.at[which, j, 1:groups, :, lanes], stat_recv.at[which, j])

    def stat(which, j, q, line):
        return stat_in[which, j, q, :, line * block : (line + 1) * block]

    squares(c)
    pl.semaphore_wait(barrier, chips + groups - 1)

    def first_block(j, carry):
        cols = cols_of(j)
        cross = dot_nt(c[...], w[cols, :])
        for at in range(0, cents, step):
            e1[at : at + step, cols] = cross[at : at + step] * slope - sb[at : at + step, :]
        send_stats(0, j, soften_block(cols, e1, None))
        return carry

    lax.fori_loop(0, groups, first_block, 0)
    ct[...] = c[...].astype(F32).T.astype(BF16)

    def combine(which, j):
        peak = stat(which, j, 0, 0)
        for q in range(1, groups):
            peak = jnp.maximum(peak, stat(which, j, q, 0))
        total = dots = 0.0
        for q in range(groups):
            part_of = jnp.exp2(stat(which, j, q, 0) - peak)
            total = total + part_of * stat(which, j, q, 1)
            if STATS[which] > 2:
                dots = dots + part_of * stat(which, j, q, 2)
        mine = jnp.exp2(stat(which, j, 0, 0) - peak)
        return mine / total, dots / total

    def first_factor(j, carry):
        wait_stats(0, j)
        row1[j, 0:1, :] = combine(0, j)[0]
        return carry

    lax.fori_loop(0, groups, first_factor, 0)

    def to_sibling(which, r, value):
        for q in range(owners):
            near_out[which, r, q] = value[q * share : (q + 1) * share]
        for q in range(PAIR):
            theirs = q * CORES + 1 - core
            start(
                near_out.at[which, r, theirs],
                near_in.at[which, r, q],
                near_send.at[which],
                near_recv.at[which, r],
                sibling,
            )

    def to_owners(which, r):
        wait(near_in.at[which, r], near_recv.at[which, r])
        if which == 0:
            wait(cnt_near.at[r], cnt_recv.at[r])
            cnt_both[r] = cnt_out[r] + cnt_near[r]

        def one(q, carry):
            total = near_out[which, r, q * CORES + core] + near_in[which, r, q]
            there = r * PAIR + q
            far = lax.rem(there - chip + chips, chips)
            slot = lax.rem(chips - far, chips)
            sum_out[which, there] = total.astype(BF16)

            @pl.when(far != 0)
            def _():
                device = {"vec": there * CORES + core}
                start(
                    sum_out.at[which, there], sum_in.at[which, slot],
                    sum_send.at[which], sum_recv.at[which], device,
                )
                if which == 0:
                    start(
                        cnt_both.at[r], cnt_in.at[slot],
                        cnt_send.at[1], cnt_recv.at[ring_y], device,
                    )

            @pl.when(far == 0)
            def _():
                sum_in[which, 0] = total.astype(BF16)
                if which == 0:
                    cnt_in[0] = cnt_both[r]

            return carry

        lax.fori_loop(0, PAIR, one, 0)

    def by_chunks(which, chunk):
        def one(t, carry):
            chunk(chunk_of(t))

            @pl.when(t > 0)
            def _():
                to_owners(which, chunk_of(t - 1))

            return carry

        lax.fori_loop(0, ring_y, one, 0)
        to_owners(which, chunk_of(ring_y - 1))

    def summed_up(which):
        wait(sum_in.at[which, 1:chips], sum_recv.at[which])
        total = sum_in[which, 0].astype(F32)
        for q in range(1, chips):
            total = total + sum_in[which, q].astype(F32)
        return total

    def to_all(which, own, everywhere):
        at = rows_from(vec)
        for far in range(1, chips):
            start(
                own, everywhere.at[at, :],
                all_send.at[which], all_recv.at[which, chips - far],
                {"vec": chip_at(far) * CORES + core},
            )
        start(own, everywhere.at[at, :], both_send.at[which], both_recv.at[which], sibling)
        everywhere[at, :] = own[...]

    def wait_all(which, everywhere):
        for k in range(1, chips):
            far = (k + 1) // 2 if k % 2 else chips - k // 2
            at = rows_from(chip_at(far) * CORES + core)
            wait(everywhere.at[at, :], all_recv.at[which, far])
            start(
                everywhere.at[at, :], everywhere.at[at, :],
                both_send.at[which], both_recv.at[which], sibling,
            )
        wait(everywhere.at[0 : chips * share, :], both_recv.at[which])

    def mass_chunk(r):
        base = r * rows_of
        for at in range(0, rows_of, step):
            here = pl.ds(pl.multiple_of(base + at, step), step)
            count = 0.0
            for j in range(groups):
                cols = slice(j * block, (j + 1) * block)
                resp = e1[here, cols] * row1[j, 0:1, :]
                r1b[here, cols] = resp.astype(BF16)
                count = count + lane_folded(resp)
            count = jnp.sum(count, axis=1, keepdims=True)
            column[at : at + step, :] = jnp.broadcast_to(count, (step, LANES))
        cnt_out[r] = column[...].T[0:1, :]
        to_sibling(0, r, dot_nn(r1b[rows_at(r), :], w[...]))
        start(cnt_out.at[r], cnt_near.at[r], cnt_send.at[0], cnt_recv.at[r], sibling)

    by_chunks(0, mass_chunk)

    wait(cnt_in.at[1:chips], cnt_recv.at[ring_y])
    count = cnt_in[0]
    for q in range(1, chips):
        count = count + cnt_in[q]
    column[...] = jnp.broadcast_to(count, (LANES, rows_of)).T
    den[...] = column[rows_from(lax.rem(vec, owners)), :] + 1e-6
    own_moved[...] = (summed_up(0) / wide(den[...], depth)).astype(BF16)
    to_all(0, own_moved, moved)
    wait_all(0, moved)

    squares(moved)

    def second_block(j, carry):
        cols = cols_of(j)
        cross = dot_nt(moved[...], w[cols, :])
        for at in range(0, cents, step):
            e2[at : at + step, cols] = cross[at : at + step] * slope - sb[at : at + step, :]
        ds[:, cols] = dot_nt(moved[...], g[cols, :])
        send_stats(1, j, soften_block(cols, e2, ds))
        return carry

    lax.fori_loop(0, groups, second_block, 0)
    mt[...] = moved[...].astype(F32).T.astype(BF16)

    def second_factor(j, carry):
        wait_stats(1, j)
        factor, dots = combine(1, j)
        row2[j, 0:1, :] = factor
        row2[j, 1:2, :] = dots
        return carry

    lax.fori_loop(0, groups, second_factor, 0)

    def cot_chunk(r):
        base = r * rows_of
        rows = rows_at(r)
        for at in range(0, rows_of, step):
            here = pl.ds(pl.multiple_of(base + at, step), step)
            total = 0.0
            for j in range(groups):
                cols = slice(j * block, (j + 1) * block)
                second = e2[here, cols] * row2[j, 0:1, :]
                r2b[here, cols] = second.astype(BF16)
                edge = second * (ds[here, cols] - row2[j, 1:2, :]) * scale
                eb[here, cols] = edge.astype(BF16)
                total = total + lane_folded(edge)
            total = jnp.sum(total, axis=1, keepdims=True)
            column[at : at + step, :] = jnp.broadcast_to(total, (step, LANES))
        cot = dot_nn(r2b[rows, :], g[...]) + dot_nn(eb[rows, :], w[...])
        to_sibling(1, r, cot - wide(column[...], depth) * moved[rows, :].astype(F32))

    by_chunks(1, cot_chunk)

    def part_block(j, carry):
        cols = cols_of(j)
        part[:, cols] = dot_nn(mt[...], eb[:, cols])
        return carry

    lax.fori_loop(0, groups, part_block, 0)

    own_mean[...] = (summed_up(1) / wide(den[...], depth)).astype(BF16)
    to_all(1, own_mean, mean)
    wait_all(1, mean)

    for at in range(0, cents, step):
        here = slice(at, at + step)
        total = jnp.sum(mean[here, :].astype(F32) * moved[here, :].astype(F32), axis=1, keepdims=True)
        sb[here, :] = jnp.broadcast_to(total, (step, block))

    in_half = groups // 2

    def block_at(u):
        h, t = u // in_half, lax.rem(u, in_half)
        far_x = lax.rem(t, PAIR)
        two_z = lax.rem(z // 2 + 1 + t // PAIR, ring_z // 2)
        return h, h * in_half + far_x * (ring_z // 2) + two_z, far_x, two_z * 2

    def third_block(u, carry):
        j = block_at(u)[1]
        cols = cols_of(j)
        cross = dot_nt(mean[...], w[cols, :])
        dots = 0.0
        for at in range(0, cents, step):
            dfirst = cross[at : at + step] - sb[at : at + step, :]
            ds[at : at + step, cols] = dfirst
            dots = dots + folded(e1[at : at + step, cols] * dfirst)
        send_stats(2, j, (jnp.sum(dots, axis=0, keepdims=True) * row1[j, 0:1, :],))
        return carry

    lax.fori_loop(0, groups, third_block, 0)
    mt[...] = mean[...].astype(F32).T.astype(BF16)

    def grad_block(u, carry):
        h, j, to_x, first_z = block_at(u)
        cols = cols_of(j)
        wait_stats(2, j)
        dots = stat(2, j, 0, 0)
        for q in range(1, groups):
            dots = dots + stat(2, j, q, 0)
        factor = row1[j, 0:1, :]
        for at in range(0, cents, step):
            first = e1[at : at + step, cols] * factor
            edge = first * (ds[at : at + step, cols] - dots) * scale
            eb[at : at + step, cols] = edge.astype(BF16)
            total = lane_folded(edge)

            @pl.when(u == 0)
            def _():
                esum[at : at + step, :] = total

            @pl.when(u != 0)
            def _():
                esum[at : at + step, :] += total

        grad = part[:, cols] + dot_nn(mt[...], r1b[:, cols]) + dot_nn(ct[...], eb[:, cols])
        grad = grad.astype(BF16)
        for q in range(2):
            to_z = first_z + q
            far = lax.rem(to_z - z + ring_z, ring_z)
            slot = lax.rem(ring_z - far, ring_z)
            mine = grad[:, q * piece : (q + 1) * piece]
            grad_out[h, to_x, to_z] = mine

            @pl.when(far != 0)
            def _():
                start(
                    grad_out.at[h, to_x, to_z], grad_in.at[h, slot, to_x],
                    grad_send, grad_recv.at[h], {"cent": x_high * ring_z + to_z},
                )

            @pl.when(far == 0)
            def _():
                grad_in[h, 0, to_x] = mine

        return carry

    lax.fori_loop(0, groups, grad_block, 0)

    other = {"cent": (1 - x_high) * ring_z + z}

    def over_z(h):
        wait(grad_in.at[h, 1:ring_z], grad_recv.at[h])

        def total(to_x):
            value = grad_in[h, 0, to_x].astype(F32)
            for q in range(1, ring_z):
                value = value + grad_in[h, q, to_x].astype(F32)
            return value

        pair_out[h] = total(1 - x_high).astype(BF16)
        start(pair_out.at[h], pair_in.at[h], pair_send, pair_recv.at[h], other)
        pair_keep[h] = total(x_high)

    def over_x(h):
        wait(pair_in.at[h], pair_recv.at[h])
        total = pair_keep[h] + pair_in[h].astype(F32)
        own_grad[h] = total.T.astype(BF16)
        rows = pl.ds(pl.multiple_of(h * half + cent * piece, piece), piece)
        for far in range(1, groups):
            start(own_grad.at[h], gw.at[rows, :], out_send, out_recv, cent_at(far))
        pltpu.make_async_copy(own_grad.at[h], gw.at[rows, :], local.at[h]).start()

    def start_chunk(r):
        rows = rows_at(r)
        total = jnp.sum(esum[rows, :], axis=1, keepdims=True)
        value = dot_nn(eb[rows, :], w[...]) - total * c[rows, :].astype(F32)
        to_sibling(2, r, value)

    over_z(0)
    by_chunks(2, start_chunk)
    over_x(0)
    over_z(1)
    own_start[...] = summed_up(2).astype(BF16)
    to_all(2, own_start, start_all)
    over_x(1)
    wait_all(2, start_all)
    result = pltpu.make_async_copy(start_all, gc, local.at[2])
    result.start()
    wait(gw.at[0 : (groups - 1) * 2 * piece, :], out_recv)
    for h in range(2):
        pltpu.make_async_copy(own_grad.at[h], gw.at[0:piece, :], local.at[h]).wait()
    result.wait()

    for which in range(3):
        lanes = slice(0, STATS[which] * block)
        wait(stat_in.at[which, :, 1:groups, :, lanes], stat_send.at[which])
        wait(near_in.at[which], near_send.at[which])
        wait(sum_in.at[which, 1:chips], sum_send.at[which])
        wait(start_all.at[0 : (chips - 1) * share, :], all_send.at[which])
        wait(start_all.at[0 : chips * share, :], both_send.at[which])
    wait(cnt_near, cnt_send.at[0])
    wait(cnt_in.at[1:chips], cnt_send.at[1])
    wait(grad_in.at[:, 1:ring_z], grad_send)
    wait(pair_in, pair_send)
    wait(gw.at[0 : (groups - 1) * 2 * piece, :], out_send)


def body(peers, groups, weights, centroids, cotangent):
    vectors, depth = weights.shape
    cents = centroids.shape[0]
    block = vectors // groups
    piece = vectors // 2 // groups
    share = cents // peers
    chips = peers // CORES
    ring_y = chips // PAIR
    ring_z = groups // PAIR
    rows_of = cents // ring_y
    owners = PAIR * CORES
    vmem = pltpu.VMEM
    dma = pltpu.SemaphoreType.DMA
    scratch = [
        vmem((cents, vectors), F32),
        vmem((cents, vectors), F32),
        vmem((cents, vectors), F32),
        vmem((cents, vectors), BF16),
        vmem((cents, vectors), BF16),
        vmem((cents, vectors), BF16),
        vmem((cents, block), F32),
        vmem((depth, cents), BF16),
        vmem((depth, cents), BF16),
        vmem((cents, depth), BF16),
        vmem((cents, depth), BF16),
        vmem((depth, vectors), F32),
        vmem((cents, LANES), F32),
        vmem((rows_of, LANES), F32),
        vmem((share, LANES), F32),
        vmem((3, groups, 1, 3 * block), F32),
        vmem((3, groups, groups, 1, 3 * block), F32),
        vmem((groups, 8, block), F32),
        vmem((groups, 8, block), F32),
        vmem((ring_y, 1, rows_of), F32),
        vmem((ring_y, 1, rows_of), F32),
        vmem((ring_y, 1, rows_of), F32),
        vmem((chips, 1, rows_of), F32),
        vmem((3, ring_y, owners, share, depth), F32),
        vmem((3, ring_y, PAIR, share, depth), F32),
        vmem((3, chips, share, depth), BF16),
        vmem((3, chips, share, depth), BF16),
        vmem((share, depth), BF16),
        vmem((share, depth), BF16),
        vmem((share, depth), BF16),
        vmem((cents, depth), BF16),
        vmem((2, PAIR, ring_z, depth, piece), BF16),
        vmem((2, ring_z, PAIR, depth, piece), BF16),
        vmem((2, depth, piece), F32),
        vmem((2, depth, piece), BF16),
        vmem((2, depth, piece), BF16),
        vmem((2, piece, depth), BF16),
        dma((3,)),
        dma((3, groups)),
        dma((3,)),
        dma((3, ring_y)),
        dma((2,)),
        dma((ring_y + 1,)),
        dma((3,)),
        dma((3,)),
        dma((3,)),
        dma((3, chips)),
        dma((3,)),
        dma((3,)),
        dma,
        dma((2,)),
        dma,
        dma((2,)),
        dma,
        dma,
        dma((3,)),
    ]
    grad_rows, start_cot = pl.pallas_call(
        functools.partial(kernel, peers, groups),
        out_shape=(
            jax.ShapeDtypeStruct((vectors, depth), BF16),
            jax.ShapeDtypeStruct((cents, depth), BF16),
        ),
        in_specs=[pl.BlockSpec(memory_space=pltpu.VMEM)] * 3,
        out_specs=[pl.BlockSpec(memory_space=pl.ANY)] * 2,
        scratch_shapes=scratch,
        compiler_params=pltpu.CompilerParams(
            collective_id=0, has_side_effects=True, vmem_limit_bytes=67043328
        ),
        name="soft_assignments",
    )(weights, centroids, cotangent)
    return grad_rows, start_cot.astype(F32)


def solution(mesh):
    return jax.shard_map(
        functools.partial(body, mesh.shape["vec"], mesh.shape["cent"]),
        mesh=mesh,
        in_specs=(P("vec", None), P("cent", None), P("vec", None)),
        out_specs=(P("vec", None), P("cent", None)),
        check_vma=False,
    )
```

```python
import functools
import math

import jax
import jax.numpy as jnp
from jax import lax
from jax.experimental import pallas as pl
from jax.experimental.pallas import tpu as pltpu
from jax.sharding import PartitionSpec as P

MESH = pl.DeviceIdType.MESH
F32 = jnp.float32
BF16 = jnp.bfloat16
CORES = 2
PAIR = 2
STATS = (2, 3, 1)
LANES = 128
LOG2E = math.log2(math.e)


def dot_nn(a, b):
    return lax.dot_general(a, b, (((1,), (0,)), ((), ())), preferred_element_type=F32)


def dot_nt(a, b):
    return lax.dot_general(a, b, (((1,), (1,)), ((), ())), preferred_element_type=F32)


def folded(x):
    return jnp.sum(x.reshape(x.shape[0] // 8, 8, x.shape[1]), axis=0)


def peaked(x):
    return jnp.max(x.reshape(x.shape[0] // 8, 8, x.shape[1]), axis=0)


def lane_folded(x):
    parts = [x[:, at : at + LANES] for at in range(0, x.shape[1], LANES)]
    return functools.reduce(jnp.add, parts)


def wide(column, width):
    return jnp.concatenate([column] * (width // LANES), axis=1)


def kernel(
    peers, groups, w_hbm, c_hbm, g_hbm, gw, gc,
    w, c, g, top_acc,
    e1, e2, ds, r1b, r2b, eb, sb, ct, mt, moved, mean, part, esum, column, den,
    stat_out, stat_in, row1, row2, cnt_out, cnt_near, cnt_both, cnt_in, near_out, near_in, sum_out, sum_in,
    own_moved, own_mean, own_start, start_all, grad_out, grad_in, pair_keep, pair_out, pair_in, own_grad,
    stat_send, stat_recv, near_send, near_recv, cnt_send, cnt_recv, sum_send, sum_recv, all_send, all_recv,
    both_send, both_recv, grad_send, grad_recv, pair_send, pair_recv, out_send, out_recv, local,
):
    vectors, depth = w.shape
    cents = c.shape[0]
    block = vectors // groups
    half = vectors // 2
    piece = half // groups
    share = cents // peers
    chips = peers // CORES
    ring_y = chips // PAIR
    ring_z = groups // PAIR
    rows_of = cents // ring_y
    owners = PAIR * CORES
    step = min(64, rows_of)
    vec = lax.axis_index("vec")
    cent = lax.axis_index("cent")
    chip, core = vec // CORES, lax.rem(vec, CORES)
    y, x_low = chip // PAIR, lax.rem(chip, PAIR)
    x_high, z = cent // ring_z, lax.rem(cent, ring_z)
    sibling = {"vec": vec + 1 - 2 * core}
    scale = 2.0 * depth ** (-0.5)
    slope = 2.0 * depth ** (-0.5) * LOG2E
    offset = depth ** (-0.5) * LOG2E

    def start(src, dst, send, recv, device):
        pltpu.make_async_remote_copy(
            src_ref=src, dst_ref=dst, send_sem=send, recv_sem=recv,
            device_id=device, device_id_type=MESH,
        ).start()

    def wait(ref, sem):
        pltpu.make_async_copy(ref, ref, sem).wait()

    def cent_at(far):
        return {"cent": lax.rem(cent + far, groups)}

    def chip_at(far):
        return lax.rem(chip + far, chips)

    def cols_of(j):
        return pl.ds(pl.multiple_of(j * block, block), block)

    def chunk_of(t):
        return lax.rem(y + 1 + t, ring_y)

    def rows_at(r):
        return pl.ds(pl.multiple_of(r * rows_of, rows_of), rows_of)

    def rows_from(owner):
        return pl.ds(pl.multiple_of(owner * share, share), share)

    loads = [
        pltpu.make_async_copy(src, dst, local.at[3 + n])
        for n, (src, dst) in enumerate(((c_hbm, c), (w_hbm, w), (g_hbm, g)))
    ]
    for load in loads:
        load.start()

    barrier = pltpu.get_barrier_semaphore()
    pl.semaphore_signal(barrier, inc=1, device_id=sibling, device_id_type=MESH)
    for far in range(1, chips):
        there = {"vec": chip_at(far) * CORES + core}
        pl.semaphore_signal(barrier, inc=1, device_id=there, device_id_type=MESH)
    for far in range(1, groups):
        pl.semaphore_signal(barrier, inc=1, device_id=cent_at(far), device_id_type=MESH)

    def expo_block(cols, top, scores, cot):
        total = dots = 0.0
        for at in range(0, cents, step):
            expo = jnp.exp2(scores[at : at + step, cols] - top)
            scores[at : at + step, cols] = expo
            total = total + folded(expo)
            if cot is not None:
                dots = dots + folded(expo * cot[at : at + step, cols])
        total = jnp.sum(total, axis=0, keepdims=True)
        if cot is None:
            return top, total
        return top, total, jnp.sum(dots, axis=0, keepdims=True)

    def send_stats(which, j, values):
        lanes = slice(0, len(values) * block)
        for line, value in enumerate(values):
            inner = slice(line * block, (line + 1) * block)
            stat_out[which, j, :, inner] = value
            stat_in[which, j, 0, :, inner] = value
        for far in range(1, groups):
            start(
                stat_out.at[which, j, :, lanes],
                stat_in.at[which, j, groups - far, :, lanes],
                stat_send.at[which],
                stat_recv.at[which, j],
                cent_at(far),
            )

    def wait_stats(which, j):
        lanes = slice(0, STATS[which] * block)
        wait(stat_in.at[which, j, 1:groups, :, lanes], stat_recv.at[which, j])

    def stat(which, j, q, line):
        return stat_in[which, j, q, :, line * block : (line + 1) * block]

    loads[0].wait()
    for at in range(0, cents, step):
        f = c[at : at + step, :].astype(F32)
        total = jnp.sum(f * f, axis=1, keepdims=True) * offset
        sb[at : at + step, :] = jnp.broadcast_to(total, (step, block))
    loads[1].wait()

    def first_scores(j):
        cols = slice(j * block, (j + 1) * block)
        cross = dot_nt(c[...], w[cols, :])
        top = None
        for at in range(0, cents, step):
            score = cross[at : at + step] * slope - sb[at : at + step, :]
            e1[at : at + step, cols] = score
            here = peaked(score)
            top = here if top is None else jnp.maximum(top, here)
        return jnp.max(top, axis=0, keepdims=True)

    tops = [first_scores(0)]
    for j in range(groups):
        if j + 1 < groups:
            tops.append(first_scores(j + 1))
        values = expo_block(slice(j * block, (j + 1) * block), tops[j], e1, None)
        if j == 0:
            pl.semaphore_wait(barrier, chips + groups - 1)
        send_stats(0, j, values)
    ct[...] = c[...].astype(F32).T.astype(BF16)

    def combine(which, j):
        peak = stat(which, j, 0, 0)
        for q in range(1, groups):
            peak = jnp.maximum(peak, stat(which, j, q, 0))
        total = dots = 0.0
        for q in range(groups):
            part_of = jnp.exp2(stat(which, j, q, 0) - peak)
            total = total + part_of * stat(which, j, q, 1)
            if STATS[which] > 2:
                dots = dots + part_of * stat(which, j, q, 2)
        mine = jnp.exp2(stat(which, j, 0, 0) - peak)
        return mine / total, dots / total

    def first_factor(j, carry):
        wait_stats(0, j)
        row1[j, 0:1, :] = combine(0, j)[0]
        return carry

    lax.fori_loop(0, groups, first_factor, 0)

    def to_sibling(which, r, value):
        for q in range(owners):
            near_out[which, r, q] = value[q * share : (q + 1) * share]
        for q in range(PAIR):
            theirs = q * CORES + 1 - core
            start(
                near_out.at[which, r, theirs],
                near_in.at[which, r, q],
                near_send.at[which],
                near_recv.at[which, r],
                sibling,
            )

    def to_owners(which, r):
        wait(near_in.at[which, r], near_recv.at[which, r])
        if which == 0:
            wait(cnt_near.at[r], cnt_recv.at[r])
            cnt_both[r] = cnt_out[r] + cnt_near[r]

        def one(q, carry):
            total = near_out[which, r, q * CORES + core] + near_in[which, r, q]
            there = r * PAIR + q
            far = lax.rem(there - chip + chips, chips)
            slot = lax.rem(chips - far, chips)
            sum_out[which, there] = total.astype(BF16)

            @pl.when(far != 0)
            def _():
                device = {"vec": there * CORES + core}
                start(
                    sum_out.at[which, there], sum_in.at[which, slot],
                    sum_send.at[which], sum_recv.at[which], device,
                )
                if which == 0:
                    start(
                        cnt_both.at[r], cnt_in.at[slot],
                        cnt_send.at[1], cnt_recv.at[ring_y], device,
                    )

            @pl.when(far == 0)
            def _():
                sum_in[which, 0] = total.astype(BF16)
                if which == 0:
                    cnt_in[0] = cnt_both[r]

            return carry

        lax.fori_loop(0, PAIR, one, 0)

    def by_chunks(which, chunk):
        def one(t, carry):
            chunk(chunk_of(t))

            @pl.when(t > 0)
            def _():
                to_owners(which, chunk_of(t - 1))

            return carry

        lax.fori_loop(0, ring_y, one, 0)
        to_owners(which, chunk_of(ring_y - 1))

    def summed_up(which):
        wait(sum_in.at[which, 1:chips], sum_recv.at[which])
        total = sum_in[which, 0].astype(F32)
        for q in range(1, chips):
            total = total + sum_in[which, q].astype(F32)
        return total

    def to_all(which, own, everywhere):
        at = rows_from(vec)
        for far in sorted(range(1, chips), key=lambda far: abs(far - chips // 2)):
            start(
                own, everywhere.at[at, :],
                all_send.at[which], all_recv.at[which, chips - far],
                {"vec": chip_at(far) * CORES + core},
            )
        start(own, everywhere.at[at, :], both_send.at[which], both_recv.at[which, 0], sibling)
        everywhere[at, :] = own[...]

    turns = sorted(range(ring_y), key=lambda d: min(d, ring_y - d))

    def sources(n):
        row = lax.rem(y + turns[n], ring_y)
        for d in range(PAIR):
            there = row * PAIR + lax.rem(x_low + d, PAIR)
            yield turns[n] or d, there, lax.rem(there - chip + chips, chips)

    def arrive(which, everywhere, n):
        for other_chip, there, far in sources(n):
            if other_chip:
                at = rows_from(there * CORES + core)
                wait(everywhere.at[at, :], all_recv.at[which, far])
                start(
                    everywhere.at[at, :], everywhere.at[at, :],
                    both_send.at[which], both_recv.at[which, far], sibling,
                )

    def gathered(which, everywhere, work):
        def finish(n):
            for _, there, far in sources(n):
                at = rows_from(there * CORES + 1 - core)
                wait(everywhere.at[at, :], both_recv.at[which, far])
            if work is not None:
                work(lax.rem(y + turns[n], ring_y))

        arrive(which, everywhere, 0)
        finish(0)
        arrive(which, everywhere, 1)
        for n in range(1, ring_y):
            if n + 1 < ring_y:
                arrive(which, everywhere, n + 1)
            finish(n)

    def mass_chunk(r):
        base = r * rows_of
        for at in range(0, rows_of, step):
            here = pl.ds(pl.multiple_of(base + at, step), step)
            count = 0.0
            for j in range(groups):
                cols = slice(j * block, (j + 1) * block)
                resp = e1[here, cols] * row1[j, 0:1, :]
                r1b[here, cols] = resp.astype(BF16)
                count = count + lane_folded(resp)
            count = jnp.sum(count, axis=1, keepdims=True)
            column[at : at + step, :] = jnp.broadcast_to(count, (step, LANES))
        cnt_out[r] = column[...].T[0:1, :]
        to_sibling(0, r, dot_nn(r1b[rows_at(r), :], w[...]))
        start(cnt_out.at[r], cnt_near.at[r], cnt_send.at[0], cnt_recv.at[r], sibling)

    by_chunks(0, mass_chunk)

    wait(cnt_in.at[1:chips], cnt_recv.at[ring_y])
    count = cnt_in[0]
    for q in range(1, chips):
        count = count + cnt_in[q]
    column[...] = jnp.broadcast_to(count, (LANES, rows_of)).T
    den[...] = column[rows_from(lax.rem(vec, owners)), :] + 1e-6
    own_moved[...] = (summed_up(0) / wide(den[...], depth)).astype(BF16)
    to_all(0, own_moved, moved)

    loads[2].wait()
    top_acc[...] = jnp.full_like(top_acc, -jnp.inf)

    def second_rows(r):
        rows = rows_at(r)
        own = moved[rows, :]
        f = own.astype(F32)
        square = jnp.sum(f * f, axis=1, keepdims=True) * offset
        for j in range(groups):
            cols = slice(j * block, (j + 1) * block)
            score = dot_nt(own, w[cols, :]) * slope - square
            e2[rows, cols] = score
            top_acc[:, cols] = jnp.maximum(top_acc[:, cols], peaked(score))
            ds[rows, cols] = dot_nt(own, g[cols, :])

    gathered(0, moved, second_rows)

    def second_block(j, carry):
        cols = cols_of(j)
        top = jnp.max(top_acc[:, cols], axis=0, keepdims=True)
        send_stats(1, j, expo_block(cols, top, e2, ds))
        return carry

    lax.fori_loop(0, groups, second_block, 0)
    mt[...] = moved[...].astype(F32).T.astype(BF16)

    def second_factor(j, carry):
        wait_stats(1, j)
        factor, dots = combine(1, j)
        row2[j, 0:1, :] = factor
        row2[j, 1:2, :] = dots
        return carry

    lax.fori_loop(0, groups, second_factor, 0)

    def cot_chunk(r):
        base = r * rows_of
        rows = rows_at(r)
        for at in range(0, rows_of, step):
            here = pl.ds(pl.multiple_of(base + at, step), step)
            total = 0.0
            for j in range(groups):
                cols = slice(j * block, (j + 1) * block)
                second = e2[here, cols] * row2[j, 0:1, :]
                r2b[here, cols] = second.astype(BF16)
                edge = second * (ds[here, cols] - row2[j, 1:2, :]) * scale
                eb[here, cols] = edge.astype(BF16)
                total = total + lane_folded(edge)
            total = jnp.sum(total, axis=1, keepdims=True)
            column[at : at + step, :] = jnp.broadcast_to(total, (step, LANES))
        cot = dot_nn(r2b[rows, :], g[...]) + dot_nn(eb[rows, :], w[...])
        to_sibling(1, r, cot - wide(column[...], depth) * moved[rows, :].astype(F32))

    by_chunks(1, cot_chunk)

    def part_block(j, carry):
        cols = pl.ds(pl.multiple_of(j * 2 * block, 2 * block), 2 * block)
        part[:, cols] = dot_nn(mt[...], eb[:, cols])
        return carry

    lax.fori_loop(0, groups // 2, part_block, 0)

    own_mean[...] = (summed_up(1) / wide(den[...], depth)).astype(BF16)
    to_all(1, own_mean, mean)

    top_acc[...] = jnp.zeros_like(top_acc)

    def third_rows(r):
        rows = rows_at(r)
        own = mean[rows, :]
        shift = jnp.sum(own.astype(F32) * moved[rows, :].astype(F32), axis=1, keepdims=True)
        for j in range(groups):
            cols = slice(j * block, (j + 1) * block)
            dfirst = dot_nt(own, w[cols, :]) - shift
            ds[rows, cols] = dfirst
            top_acc[:, cols] += folded(e1[rows, cols] * dfirst)

    gathered(1, mean, third_rows)
    for j in range(groups):
        cols = slice(j * block, (j + 1) * block)
        send_stats(2, j, (jnp.sum(top_acc[:, cols], axis=0, keepdims=True) * row1[j, 0:1, :],))
    mt[...] = mean[...].astype(F32).T.astype(BF16)

    def mean_block(j, carry):
        cols = pl.ds(pl.multiple_of(j * 2 * block, 2 * block), 2 * block)
        part[:, cols] += dot_nn(mt[...], r1b[:, cols])
        return carry

    lax.fori_loop(0, groups // 2, mean_block, 0)

    in_half = groups // 2

    def block_at(u):
        h, t = u // in_half, lax.rem(u, in_half)
        far_x = lax.rem(t, PAIR)
        two_z = lax.rem(z // 2 + 1 + t // PAIR, ring_z // 2)
        return h, h * in_half + far_x * (ring_z // 2) + two_z, far_x, two_z * 2

    def grad_block(u, carry):
        h, j, to_x, first_z = block_at(u)
        cols = cols_of(j)
        wait_stats(2, j)
        dots = stat(2, j, 0, 0)
        for q in range(1, groups):
            dots = dots + stat(2, j, q, 0)
        factor = row1[j, 0:1, :]
        for at in range(0, cents, step):
            first = e1[at : at + step, cols] * factor
            edge = first * (ds[at : at + step, cols] - dots) * scale
            eb[at : at + step, cols] = edge.astype(BF16)
            total = lane_folded(edge)

            @pl.when(u == 0)
            def _():
                esum[at : at + step, :] = total

            @pl.when(u != 0)
            def _():
                esum[at : at + step, :] += total

        grad = part[:, cols] + dot_nn(ct[...], eb[:, cols])
        grad = grad.astype(BF16)
        for q in range(2):
            to_z = first_z + q
            far = lax.rem(to_z - z + ring_z, ring_z)
            slot = lax.rem(ring_z - far, ring_z)
            mine = grad[:, q * piece : (q + 1) * piece]
            grad_out[h, to_x, to_z] = mine

            @pl.when(far != 0)
            def _():
                start(
                    grad_out.at[h, to_x, to_z], grad_in.at[h, slot, to_x],
                    grad_send, grad_recv.at[h], {"cent": x_high * ring_z + to_z},
                )

            @pl.when(far == 0)
            def _():
                grad_in[h, 0, to_x] = mine

        return carry

    lax.fori_loop(0, groups, grad_block, 0)

    other = {"cent": (1 - x_high) * ring_z + z}

    def over_z(h):
        wait(grad_in.at[h, 1:ring_z], grad_recv.at[h])

        def total(to_x):
            value = grad_in[h, 0, to_x].astype(F32)
            for q in range(1, ring_z):
                value = value + grad_in[h, q, to_x].astype(F32)
            return value

        pair_out[h] = total(1 - x_high).astype(BF16)
        start(pair_out.at[h], pair_in.at[h], pair_send, pair_recv.at[h], other)
        pair_keep[h] = total(x_high)

    def over_x(h):
        wait(pair_in.at[h], pair_recv.at[h])
        total = pair_keep[h] + pair_in[h].astype(F32)
        own_grad[h] = total.T.astype(BF16)
        rows = pl.ds(pl.multiple_of(h * half + cent * piece, piece), piece)
        for far in range(1, groups):
            start(own_grad.at[h], gw.at[rows, :], out_send, out_recv, cent_at(far))
        pltpu.make_async_copy(own_grad.at[h], gw.at[rows, :], local.at[h]).start()

    def start_chunk(r):
        rows = rows_at(r)
        total = jnp.sum(esum[rows, :], axis=1, keepdims=True)
        value = dot_nn(eb[rows, :], w[...]) - total * c[rows, :].astype(F32)
        to_sibling(2, r, value)

    over_z(0)
    by_chunks(2, start_chunk)
    over_x(0)
    over_z(1)
    own_start[...] = summed_up(2).astype(BF16)
    to_all(2, own_start, start_all)
    over_x(1)
    gathered(2, start_all, None)
    result = pltpu.make_async_copy(start_all, gc, local.at[2])
    result.start()
    wait(gw.at[0 : (groups - 1) * 2 * piece, :], out_recv)
    for h in range(2):
        pltpu.make_async_copy(own_grad.at[h], gw.at[0:piece, :], local.at[h]).wait()
    result.wait()

    for which in range(3):
        lanes = slice(0, STATS[which] * block)
        wait(stat_in.at[which, :, 1:groups, :, lanes], stat_send.at[which])
        wait(near_in.at[which], near_send.at[which])
        wait(sum_in.at[which, 1:chips], sum_send.at[which])
        wait(start_all.at[0 : (chips - 1) * share, :], all_send.at[which])
        wait(start_all.at[0 : chips * share, :], both_send.at[which])
    wait(cnt_near, cnt_send.at[0])
    wait(cnt_in.at[1:chips], cnt_send.at[1])
    wait(grad_in.at[:, 1:ring_z], grad_send)
    wait(pair_in, pair_send)
    wait(gw.at[0 : (groups - 1) * 2 * piece, :], out_send)


def body(peers, groups, weights, centroids, cotangent):
    vectors, depth = weights.shape
    cents = centroids.shape[0]
    block = vectors // groups
    piece = vectors // 2 // groups
    share = cents // peers
    chips = peers // CORES
    ring_y = chips // PAIR
    ring_z = groups // PAIR
    rows_of = cents // ring_y
    owners = PAIR * CORES
    vmem = pltpu.VMEM
    dma = pltpu.SemaphoreType.DMA
    scratch = [
        vmem((vectors, depth), BF16),
        vmem((cents, depth), BF16),
        vmem((vectors, depth), BF16),
        vmem((8, vectors), F32),
        vmem((cents, vectors), F32),
        vmem((cents, vectors), F32),
        vmem((cents, vectors), F32),
        vmem((cents, vectors), BF16),
        vmem((cents, vectors), BF16),
        vmem((cents, vectors), BF16),
        vmem((cents, block), F32),
        vmem((depth, cents), BF16),
        vmem((depth, cents), BF16),
        vmem((cents, depth), BF16),
        vmem((cents, depth), BF16),
        vmem((depth, vectors), F32),
        vmem((cents, LANES), F32),
        vmem((rows_of, LANES), F32),
        vmem((share, LANES), F32),
        vmem((3, groups, 1, 3 * block), F32),
        vmem((3, groups, groups, 1, 3 * block), F32),
        vmem((groups, 8, block), F32),
        vmem((groups, 8, block), F32),
        vmem((ring_y, 1, rows_of), F32),
        vmem((ring_y, 1, rows_of), F32),
        vmem((ring_y, 1, rows_of), F32),
        vmem((chips, 1, rows_of), F32),
        vmem((3, ring_y, owners, share, depth), F32),
        vmem((3, ring_y, PAIR, share, depth), F32),
        vmem((3, chips, share, depth), BF16),
        vmem((3, chips, share, depth), BF16),
        vmem((share, depth), BF16),
        vmem((share, depth), BF16),
        vmem((share, depth), BF16),
        vmem((cents, depth), BF16),
        vmem((2, PAIR, ring_z, depth, piece), BF16),
        vmem((2, ring_z, PAIR, depth, piece), BF16),
        vmem((2, depth, piece), F32),
        vmem((2, depth, piece), BF16),
        vmem((2, depth, piece), BF16),
        vmem((2, piece, depth), BF16),
        dma((3,)),
        dma((3, groups)),
        dma((3,)),
        dma((3, ring_y)),
        dma((2,)),
        dma((ring_y + 1,)),
        dma((3,)),
        dma((3,)),
        dma((3,)),
        dma((3, chips)),
        dma((3,)),
        dma((3, chips)),
        dma,
        dma((2,)),
        dma,
        dma((2,)),
        dma,
        dma,
        dma((6,)),
    ]
    grad_rows, start_cot = pl.pallas_call(
        functools.partial(kernel, peers, groups),
        out_shape=(
            jax.ShapeDtypeStruct((vectors, depth), BF16),
            jax.ShapeDtypeStruct((cents, depth), BF16),
        ),
        in_specs=[pl.BlockSpec(memory_space=pl.ANY)] * 3,
        out_specs=[pl.BlockSpec(memory_space=pl.ANY)] * 2,
        scratch_shapes=scratch,
        compiler_params=pltpu.CompilerParams(
            collective_id=0, has_side_effects=True, vmem_limit_bytes=67043328
        ),
        name="soft_assignments",
    )(weights, centroids, cotangent)
    return grad_rows, start_cot.astype(F32)


def solution(mesh):
    return jax.shard_map(
        functools.partial(body, mesh.shape["vec"], mesh.shape["cent"]),
        mesh=mesh,
        in_specs=(P("vec", None), P("cent", None), P("vec", None)),
        out_specs=(P("vec", None), P("cent", None)),
        check_vma=False,
    )
```

```python
import functools
import math

import jax
import jax.numpy as jnp
from jax import lax
from jax.experimental import pallas as pl
from jax.experimental.pallas import tpu as pltpu
from jax.sharding import PartitionSpec as P

MESH = pl.DeviceIdType.MESH
F32 = jnp.float32
BF16 = jnp.bfloat16
CORES = 2
PAIR = 2
STATS = (2, 3, 1)
LANES = 128
LOG2E = math.log2(math.e)


def dot_nn(a, b):
    return lax.dot_general(a, b, (((1,), (0,)), ((), ())), preferred_element_type=F32)


def dot_nt(a, b):
    return lax.dot_general(a, b, (((1,), (1,)), ((), ())), preferred_element_type=F32)


def folded(x):
    return jnp.sum(x.reshape(x.shape[0] // 8, 8, x.shape[1]), axis=0)


def peaked(x):
    return jnp.max(x.reshape(x.shape[0] // 8, 8, x.shape[1]), axis=0)


def lane_folded(x):
    parts = [x[:, at : at + LANES] for at in range(0, x.shape[1], LANES)]
    return functools.reduce(jnp.add, parts)


def wide(column, width):
    return jnp.concatenate([column] * (width // LANES), axis=1)


def kernel(
    peers, groups, w_hbm, c_hbm, g_hbm, gw, gc,
    w, c, g, top_acc,
    e1, e2, ds, r1b, r2b, eb, sb, ct, mt, moved, mean, part, esum, column, den,
    stat_out, stat_in, row1, row2, cnt_out, cnt_near, cnt_both, cnt_in, near_out, near_in, sum_out, sum_in,
    own_moved, own_mean, own_start, start_all, grad_out, grad_in, pair_out, pair_in, own_grad,
    stat_send, stat_recv, near_send, near_recv, cnt_send, cnt_recv, sum_send, sum_recv, all_send, all_recv,
    both_send, both_recv, grad_send, grad_recv, pair_send, pair_recv, out_send, out_recv, local,
):
    vectors, depth = w.shape
    cents = c.shape[0]
    block = vectors // groups
    half = vectors // 2
    piece = half // groups
    share = cents // peers
    chips = peers // CORES
    ring_y = chips // PAIR
    ring_z = groups // PAIR
    rows_of = cents // ring_y
    owners = PAIR * CORES
    step = min(64, rows_of)
    vec = lax.axis_index("vec")
    cent = lax.axis_index("cent")
    chip, core = vec // CORES, lax.rem(vec, CORES)
    y, x_low = chip // PAIR, lax.rem(chip, PAIR)
    x_high, z = cent // ring_z, lax.rem(cent, ring_z)
    sibling = {"vec": vec + 1 - 2 * core}
    scale = 2.0 * depth ** (-0.5)
    slope = 2.0 * depth ** (-0.5) * LOG2E
    offset = depth ** (-0.5) * LOG2E

    def start(src, dst, send, recv, device):
        pltpu.make_async_remote_copy(
            src_ref=src, dst_ref=dst, send_sem=send, recv_sem=recv,
            device_id=device, device_id_type=MESH,
        ).start()

    def wait(ref, sem):
        pltpu.make_async_copy(ref, ref, sem).wait()

    def cent_at(far):
        return {"cent": lax.rem(cent + far, groups)}

    def chip_at(far):
        return lax.rem(chip + far, chips)

    def cols_of(j):
        return pl.ds(pl.multiple_of(j * block, block), block)

    def chunk_of(t):
        return lax.rem(y + 1 + t, ring_y)

    def rows_at(r):
        return pl.ds(pl.multiple_of(r * rows_of, rows_of), rows_of)

    def rows_from(owner):
        return pl.ds(pl.multiple_of(owner * share, share), share)

    loads = [
        pltpu.make_async_copy(src, dst, local.at[3 + n])
        for n, (src, dst) in enumerate(((c_hbm, c), (w_hbm, w), (g_hbm, g)))
    ]
    for load in loads:
        load.start()

    barrier = pltpu.get_barrier_semaphore()
    pl.semaphore_signal(barrier, inc=1, device_id=sibling, device_id_type=MESH)
    for far in range(1, chips):
        there = {"vec": chip_at(far) * CORES + core}
        pl.semaphore_signal(barrier, inc=1, device_id=there, device_id_type=MESH)
    for far in range(1, groups):
        pl.semaphore_signal(barrier, inc=1, device_id=cent_at(far), device_id_type=MESH)

    def expo_block(cols, top, scores, cot):
        total = dots = 0.0
        for at in range(0, cents, step):
            expo = jnp.exp2(scores[at : at + step, cols] - top)
            scores[at : at + step, cols] = expo
            total = total + folded(expo)
            if cot is not None:
                dots = dots + folded(expo * cot[at : at + step, cols])
        total = jnp.sum(total, axis=0, keepdims=True)
        if cot is None:
            return top, total
        return top, total, jnp.sum(dots, axis=0, keepdims=True)

    def keep_stats(which, j, values):
        for line, value in enumerate(values):
            inner = slice(line * block, (line + 1) * block)
            stat_out[which, j, :, inner] = value
            stat_in[which, j, 0, :, inner] = value

    def send_stats(which, j):
        lanes = slice(0, STATS[which] * block)
        for far in range(1, groups):
            start(
                stat_out.at[which, j, :, lanes],
                stat_in.at[which, j, groups - far, :, lanes],
                stat_send.at[which],
                stat_recv.at[which, j],
                cent_at(far),
            )

    def wait_stats(which, j):
        lanes = slice(0, STATS[which] * block)
        wait(stat_in.at[which, j, 1:groups, :, lanes], stat_recv.at[which, j])

    def stat(which, j, q, line):
        return stat_in[which, j, q, :, line * block : (line + 1) * block]

    loads[0].wait()
    for at in range(0, cents, step):
        f = c[at : at + step, :].astype(F32)
        total = jnp.sum(f * f, axis=1, keepdims=True) * offset
        sb[at : at + step, :] = jnp.broadcast_to(total, (step, block))
    loads[1].wait()

    def first_scores(j):
        cols = slice(j * block, (j + 1) * block)
        cross = dot_nt(c[...], w[cols, :])
        top = None
        for at in range(0, cents, step):
            score = cross[at : at + step] * slope - sb[at : at + step, :]
            e1[at : at + step, cols] = score
            here = peaked(score)
            top = here if top is None else jnp.maximum(top, here)
        return jnp.max(top, axis=0, keepdims=True)

    tops = [first_scores(0)]
    for j in range(groups):
        if j + 1 < groups:
            tops.append(first_scores(j + 1))
        keep_stats(0, j, expo_block(slice(j * block, (j + 1) * block), tops[j], e1, None))
    pl.semaphore_wait(barrier, chips + groups - 1)
    for j in range(groups):
        send_stats(0, j)
    ct[...] = c[...].astype(F32).T.astype(BF16)

    def combine(which, j):
        peak = stat(which, j, 0, 0)
        for q in range(1, groups):
            peak = jnp.maximum(peak, stat(which, j, q, 0))
        total = dots = 0.0
        for q in range(groups):
            part_of = jnp.exp2(stat(which, j, q, 0) - peak)
            total = total + part_of * stat(which, j, q, 1)
            if STATS[which] > 2:
                dots = dots + part_of * stat(which, j, q, 2)
        mine = jnp.exp2(stat(which, j, 0, 0) - peak)
        return mine / total, dots / total

    for j in range(groups):
        wait_stats(0, j)
    for j in range(groups):
        row1[j, 0:1, :] = combine(0, j)[0]

    def to_sibling(which, r, value):
        for q in range(owners):
            near_out[which, r, q] = value[q * share : (q + 1) * share]
        for q in range(PAIR):
            theirs = q * CORES + 1 - core
            start(
                near_out.at[which, r, theirs],
                near_in.at[which, r, q],
                near_send.at[which],
                near_recv.at[which, r],
                sibling,
            )

    def to_owners(which, r):
        wait(near_in.at[which, r], near_recv.at[which, r])
        if which == 0:
            wait(cnt_near.at[r], cnt_recv.at[r])
            cnt_both[r] = cnt_out[r] + cnt_near[r]

        def one(q, carry):
            total = near_out[which, r, q * CORES + core] + near_in[which, r, q]
            there = r * PAIR + q
            far = lax.rem(there - chip + chips, chips)
            slot = lax.rem(chips - far, chips)
            sum_out[which, there] = total.astype(BF16)

            @pl.when(far != 0)
            def _():
                device = {"vec": there * CORES + core}
                start(
                    sum_out.at[which, there], sum_in.at[which, slot],
                    sum_send.at[which], sum_recv.at[which], device,
                )
                if which == 0:
                    start(
                        cnt_both.at[r], cnt_in.at[slot],
                        cnt_send.at[1], cnt_recv.at[ring_y], device,
                    )

            @pl.when(far == 0)
            def _():
                sum_in[which, 0] = total.astype(BF16)
                if which == 0:
                    cnt_in[0] = cnt_both[r]

            return carry

        lax.fori_loop(0, PAIR, one, 0)

    def by_chunks(which, chunk):
        def one(t, carry):
            chunk(chunk_of(t))

            @pl.when(t > 0)
            def _():
                to_owners(which, chunk_of(t - 1))

            return carry

        lax.fori_loop(0, ring_y, one, 0)
        to_owners(which, chunk_of(ring_y - 1))

    def summed_up(which):
        wait(sum_in.at[which, 1:chips], sum_recv.at[which])
        total = sum_in[which, 0].astype(F32)
        for q in range(1, chips):
            total = total + sum_in[which, q].astype(F32)
        return total

    turns = sorted(range(ring_y), key=lambda d: min(d, ring_y - d))

    def sources(n):
        row = lax.rem(y + turns[n], ring_y)
        for d in range(PAIR):
            there = row * PAIR + lax.rem(x_low + d, PAIR)
            yield turns[n] or d, there, lax.rem(there - chip + chips, chips)

    def to_all(which, own, everywhere):
        at = rows_from(vec)
        for n in range(ring_y):
            for other_chip, there, far in sources(n):
                if other_chip:
                    start(
                        own, everywhere.at[at, :],
                        all_send.at[which], all_recv.at[which, lax.rem(chips - far, chips)],
                        {"vec": there * CORES + core},
                    )
                else:
                    start(own, everywhere.at[at, :], both_send.at[which], both_recv.at[which, 0], sibling)
        everywhere[at, :] = own[...]

    def arrive(which, everywhere, n):
        for other_chip, there, far in sources(n):
            if other_chip:
                at = rows_from(there * CORES + core)
                wait(everywhere.at[at, :], all_recv.at[which, far])
                start(
                    everywhere.at[at, :], everywhere.at[at, :],
                    both_send.at[which], both_recv.at[which, far], sibling,
                )

    def gathered(which, everywhere, work):
        def finish(n):
            for _, there, far in sources(n):
                at = rows_from(there * CORES + 1 - core)
                wait(everywhere.at[at, :], both_recv.at[which, far])
            if work is not None:
                work(lax.rem(y + turns[n], ring_y))

        arrive(which, everywhere, 0)
        finish(0)
        arrive(which, everywhere, 1)
        for n in range(1, ring_y):
            if n + 1 < ring_y:
                arrive(which, everywhere, n + 1)
            finish(n)

    def mass_chunk(r):
        base = r * rows_of
        ats = range(0, rows_of, step)
        counts = [0.0] * len(ats)
        for j in range(groups):
            cols = slice(j * block, (j + 1) * block)
            for n, at in enumerate(ats):
                here = pl.ds(pl.multiple_of(base + at, step), step)
                resp = e1[here, cols] * row1[j, 0:1, :]
                r1b[here, cols] = resp.astype(BF16)
                counts[n] = counts[n] + lane_folded(resp)
        for n, at in enumerate(ats):
            count = jnp.sum(counts[n], axis=1, keepdims=True)
            column[at : at + step, :] = jnp.broadcast_to(count, (step, LANES))
        cnt_out[r] = column[...].T[0:1, :]
        to_sibling(0, r, dot_nn(r1b[rows_at(r), :], w[...]))
        start(cnt_out.at[r], cnt_near.at[r], cnt_send.at[0], cnt_recv.at[r], sibling)

    by_chunks(0, mass_chunk)

    wait(cnt_in.at[1:chips], cnt_recv.at[ring_y])
    count = cnt_in[0]
    for q in range(1, chips):
        count = count + cnt_in[q]
    column[...] = jnp.broadcast_to(count, (LANES, rows_of)).T
    den[...] = column[rows_from(lax.rem(vec, owners)), :] + 1e-6
    own_moved[...] = (summed_up(0) / wide(den[...], depth)).astype(BF16)
    to_all(0, own_moved, moved)

    loads[2].wait()
    top_acc[...] = jnp.full_like(top_acc, -jnp.inf)

    def second_rows(r):
        rows = rows_at(r)
        own = moved[rows, :]
        f = own.astype(F32)
        square = jnp.sum(f * f, axis=1, keepdims=True) * offset
        for j in range(groups):
            cols = slice(j * block, (j + 1) * block)
            score = dot_nt(own, w[cols, :]) * slope - square
            e2[rows, cols] = score
            top_acc[:, cols] = jnp.maximum(top_acc[:, cols], peaked(score))
            ds[rows, cols] = dot_nt(own, g[cols, :])

    gathered(0, moved, second_rows)

    def second_block(j, carry):
        cols = cols_of(j)
        top = jnp.max(top_acc[:, cols], axis=0, keepdims=True)
        keep_stats(1, j, expo_block(cols, top, e2, ds))
        send_stats(1, j)
        return carry

    lax.fori_loop(0, groups, second_block, 0)
    mt[...] = moved[...].astype(F32).T.astype(BF16)

    for j in range(groups):
        wait_stats(1, j)
    for j in range(groups):
        factor, dots = combine(1, j)
        row2[j, 0:1, :] = factor
        row2[j, 1:2, :] = dots

    def cot_chunk(r):
        base = r * rows_of
        rows = rows_at(r)
        ats = range(0, rows_of, step)
        totals = [0.0] * len(ats)
        for j in range(groups):
            cols = slice(j * block, (j + 1) * block)
            for n, at in enumerate(ats):
                here = pl.ds(pl.multiple_of(base + at, step), step)
                second = e2[here, cols] * row2[j, 0:1, :]
                r2b[here, cols] = second.astype(BF16)
                edge = second * (ds[here, cols] - row2[j, 1:2, :]) * scale
                eb[here, cols] = edge.astype(BF16)
                totals[n] = totals[n] + lane_folded(edge)
        for n, at in enumerate(ats):
            total = jnp.sum(totals[n], axis=1, keepdims=True)
            column[at : at + step, :] = jnp.broadcast_to(total, (step, LANES))
        cot = dot_nn(r2b[rows, :], g[...]) + dot_nn(eb[rows, :], w[...])
        to_sibling(1, r, cot - wide(column[...], depth) * moved[rows, :].astype(F32))

    by_chunks(1, cot_chunk)

    def part_block(j, carry):
        cols = pl.ds(pl.multiple_of(j * 2 * block, 2 * block), 2 * block)
        part[:, cols] = dot_nn(mt[...], eb[:, cols])
        return carry

    lax.fori_loop(0, groups // 2, part_block, 0)

    own_mean[...] = (summed_up(1) / wide(den[...], depth)).astype(BF16)
    to_all(1, own_mean, mean)

    top_acc[...] = jnp.zeros_like(top_acc)

    def third_rows(r):
        rows = rows_at(r)
        own = mean[rows, :]
        shift = jnp.sum(own.astype(F32) * moved[rows, :].astype(F32), axis=1, keepdims=True)
        for j in range(groups):
            cols = slice(j * block, (j + 1) * block)
            dfirst = dot_nt(own, w[cols, :]) - shift
            ds[rows, cols] = dfirst
            top_acc[:, cols] += folded(e1[rows, cols] * dfirst)

    gathered(1, mean, third_rows)
    for j in range(groups):
        cols = slice(j * block, (j + 1) * block)
        keep_stats(2, j, (jnp.sum(top_acc[:, cols], axis=0, keepdims=True) * row1[j, 0:1, :],))
        send_stats(2, j)
    mt[...] = mean[...].astype(F32).T.astype(BF16)

    def mean_block(j, carry):
        cols = pl.ds(pl.multiple_of(j * 2 * block, 2 * block), 2 * block)
        part[:, cols] += dot_nn(mt[...], r1b[:, cols])
        return carry

    lax.fori_loop(0, groups // 2, mean_block, 0)

    in_half = groups // 2

    def block_at(u):
        h, t = u // in_half, lax.rem(u, in_half)
        far_x = lax.rem(t, PAIR)
        two_z = lax.rem(z // 2 + 1 + t // PAIR, ring_z // 2)
        return h, h * in_half + far_x * (ring_z // 2) + two_z, far_x, two_z * 2

    def grad_block(u, carry):
        h, j, to_x, first_z = block_at(u)
        cols = cols_of(j)
        wait_stats(2, j)
        dots = stat(2, j, 0, 0)
        for q in range(1, groups):
            dots = dots + stat(2, j, q, 0)
        factor = row1[j, 0:1, :]
        for at in range(0, cents, step):
            first = e1[at : at + step, cols] * factor
            edge = first * (ds[at : at + step, cols] - dots) * scale
            eb[at : at + step, cols] = edge.astype(BF16)
            total = lane_folded(edge)

            @pl.when(u == 0)
            def _():
                esum[at : at + step, :] = total

            @pl.when(u != 0)
            def _():
                esum[at : at + step, :] += total

        grad = part[:, cols] + dot_nn(ct[...], eb[:, cols])
        grad = grad.astype(BF16)
        for q in range(2):
            to_z = first_z + q
            far = lax.rem(to_z - z + ring_z, ring_z)
            slot = lax.rem(ring_z - far, ring_z)
            mine = grad[:, q * piece : (q + 1) * piece]
            grad_out[h, to_x, to_z] = mine

            @pl.when(far != 0)
            def _():
                start(
                    grad_out.at[h, to_x, to_z], grad_in.at[h, slot, to_x],
                    grad_send, grad_recv.at[h], {"cent": x_high * ring_z + to_z},
                )

            @pl.when(far == 0)
            def _():
                grad_in[h, 0, to_x] = mine

        return carry

    lax.fori_loop(0, groups, grad_block, 0)

    other = {"cent": (1 - x_high) * ring_z + z}

    part_d = depth // 2

    def over_z(h, n):
        if n == 0:
            wait(grad_in.at[h, 1:ring_z], grad_recv.at[h])
        for to_x in range(PAIR):
            inner = slice(n * part_d, (n + 1) * part_d)
            total = grad_in[h, 0, to_x, inner, :].astype(F32)
            for q in range(1, ring_z):
                total = total + grad_in[h, q, to_x, inner, :].astype(F32)
            pair_out[h, n, to_x] = total.astype(BF16)
        start(pair_out.at[h, n], pair_in.at[h, n], pair_send, pair_recv.at[h, n], other)

    def grad_place(h, n, to_x):
        rows = h * half + (to_x * ring_z + z) * piece
        return gw.at[pl.ds(pl.multiple_of(rows, piece), piece), n * part_d : (n + 1) * part_d]

    def over_x(h, n):
        wait(pair_in.at[h, n], pair_recv.at[h, n])
        for to_x in range(PAIR):
            total = pair_out[h, n, to_x].astype(F32) + pair_in[h, n, to_x].astype(F32)
            own_grad[h, n, to_x] = total.T.astype(BF16)
        for to_x in range(PAIR):
            place = grad_place(h, n, to_x)
            for far in range(1, ring_z):
                there = {"cent": x_high * ring_z + lax.rem(z + far, ring_z)}
                start(own_grad.at[h, n, to_x], place, out_send, out_recv, there)
            pltpu.make_async_copy(own_grad.at[h, n, to_x], place, local.at[h]).start()

    def start_chunk(r):
        rows = rows_at(r)
        total = jnp.sum(esum[rows, :], axis=1, keepdims=True)
        value = dot_nn(eb[rows, :], w[...]) - total * c[rows, :].astype(F32)
        to_sibling(2, r, value)

    over_z(0, 0)
    over_z(0, 1)
    by_chunks(2, start_chunk)
    over_x(0, 0)
    over_x(0, 1)
    over_z(1, 0)
    over_z(1, 1)
    own_start[...] = summed_up(2).astype(BF16)
    to_all(2, own_start, start_all)
    over_x(1, 0)
    over_x(1, 1)
    gathered(2, start_all, None)
    result = pltpu.make_async_copy(start_all, gc, local.at[2])
    result.start()
    wait(gw.at[0 : (ring_z - 1) * 2 * PAIR * piece, :], out_recv)
    for h in range(2):
        wait(gw.at[0 : PAIR * piece, :], local.at[h])
    result.wait()

    for which in range(3):
        lanes = slice(0, STATS[which] * block)
        wait(stat_in.at[which, :, 1:groups, :, lanes], stat_send.at[which])
        wait(near_in.at[which], near_send.at[which])
        wait(sum_in.at[which, 1:chips], sum_send.at[which])
        wait(start_all.at[0 : (chips - 1) * share, :], all_send.at[which])
        wait(start_all.at[0 : chips * share, :], both_send.at[which])
    wait(cnt_near, cnt_send.at[0])
    wait(cnt_in.at[1:chips], cnt_send.at[1])
    wait(grad_in.at[:, 1:ring_z], grad_send)
    wait(pair_in, pair_send)
    wait(gw.at[0 : (ring_z - 1) * 2 * PAIR * piece, :], out_send)


def body(peers, groups, weights, centroids, cotangent):
    vectors, depth = weights.shape
    cents = centroids.shape[0]
    block = vectors // groups
    piece = vectors // 2 // groups
    share = cents // peers
    chips = peers // CORES
    ring_y = chips // PAIR
    ring_z = groups // PAIR
    rows_of = cents // ring_y
    owners = PAIR * CORES
    vmem = pltpu.VMEM
    dma = pltpu.SemaphoreType.DMA
    scratch = [
        vmem((vectors, depth), BF16),
        vmem((cents, depth), BF16),
        vmem((vectors, depth), BF16),
        vmem((8, vectors), F32),
        vmem((cents, vectors), F32),
        vmem((cents, vectors), F32),
        vmem((cents, vectors), F32),
        vmem((cents, vectors), BF16),
        vmem((cents, vectors), BF16),
        vmem((cents, vectors), BF16),
        vmem((cents, block), F32),
        vmem((depth, cents), BF16),
        vmem((depth, cents), BF16),
        vmem((cents, depth), BF16),
        vmem((cents, depth), BF16),
        vmem((depth, vectors), F32),
        vmem((cents, LANES), F32),
        vmem((rows_of, LANES), F32),
        vmem((share, LANES), F32),
        vmem((3, groups, 1, 3 * block), F32),
        vmem((3, groups, groups, 1, 3 * block), F32),
        vmem((groups, 8, block), F32),
        vmem((groups, 8, block), F32),
        vmem((ring_y, 1, rows_of), F32),
        vmem((ring_y, 1, rows_of), F32),
        vmem((ring_y, 1, rows_of), F32),
        vmem((chips, 1, rows_of), F32),
        vmem((3, ring_y, owners, share, depth), F32),
        vmem((3, ring_y, PAIR, share, depth), F32),
        vmem((3, chips, share, depth), BF16),
        vmem((3, chips, share, depth), BF16),
        vmem((share, depth), BF16),
        vmem((share, depth), BF16),
        vmem((share, depth), BF16),
        vmem((cents, depth), BF16),
        vmem((2, PAIR, ring_z, depth, piece), BF16),
        vmem((2, ring_z, PAIR, depth, piece), BF16),
        vmem((2, 2, PAIR, depth // 2, piece), BF16),
        vmem((2, 2, PAIR, depth // 2, piece), BF16),
        vmem((2, 2, PAIR, piece, depth // 2), BF16),
        dma((3,)),
        dma((3, groups)),
        dma((3,)),
        dma((3, ring_y)),
        dma((2,)),
        dma((ring_y + 1,)),
        dma((3,)),
        dma((3,)),
        dma((3,)),
        dma((3, chips)),
        dma((3,)),
        dma((3, chips)),
        dma,
        dma((2,)),
        dma,
        dma((2, 2)),
        dma,
        dma,
        dma((6,)),
    ]
    grad_rows, start_cot = pl.pallas_call(
        functools.partial(kernel, peers, groups),
        out_shape=(
            jax.ShapeDtypeStruct((vectors, depth), BF16),
            jax.ShapeDtypeStruct((cents, depth), BF16),
        ),
        in_specs=[pl.BlockSpec(memory_space=pl.ANY)] * 3,
        out_specs=[pl.BlockSpec(memory_space=pl.ANY)] * 2,
        scratch_shapes=scratch,
        compiler_params=pltpu.CompilerParams(
            collective_id=0, has_side_effects=True, vmem_limit_bytes=67043328
        ),
        name="soft_assignments",
    )(weights, centroids, cotangent)
    return grad_rows, start_cot.astype(F32)


def solution(mesh):
    return jax.shard_map(
        functools.partial(body, mesh.shape["vec"], mesh.shape["cent"]),
        mesh=mesh,
        in_specs=(P("vec", None), P("cent", None), P("vec", None)),
        out_specs=(P("vec", None), P("cent", None)),
        check_vma=False,
    )
```

```python
import functools
import math

import jax
import jax.numpy as jnp
from jax import lax
from jax.experimental import pallas as pl
from jax.experimental.pallas import tpu as pltpu
from jax.sharding import PartitionSpec as P

MESH = pl.DeviceIdType.MESH
F32 = jnp.float32
BF16 = jnp.bfloat16
CORES = 2
PAIR = 2
STATS = (2, 3, 1)
LANES = 128
LOG2E = math.log2(math.e)


def dot_nn(a, b):
    return lax.dot_general(a, b, (((1,), (0,)), ((), ())), preferred_element_type=F32)


def dot_nt(a, b):
    return lax.dot_general(a, b, (((1,), (1,)), ((), ())), preferred_element_type=F32)


def folded(x):
    return jnp.sum(x.reshape(x.shape[0] // 8, 8, x.shape[1]), axis=0)


def peaked(x):
    return jnp.max(x.reshape(x.shape[0] // 8, 8, x.shape[1]), axis=0)


def lane_folded(x):
    parts = [x[:, at : at + LANES] for at in range(0, x.shape[1], LANES)]
    return functools.reduce(jnp.add, parts)


def wide(column, width):
    return jnp.concatenate([column] * (width // LANES), axis=1)


def kernel(
    peers, groups, w_hbm, c_hbm, g_hbm, gw, gc,
    w, c, g, top_acc,
    e1, e2, ds, r1b, r2b, eb, sb, ct, mt, moved, mean, part, esum, column, den,
    stat_out, stat_in, row1, row2, cnt_out, cnt_near, cnt_both, cnt_in, near_out, near_in, sum_out, sum_in,
    own_moved, own_mean, own_start, start_all, grad_out, grad_in, pair_out, pair_in, own_grad,
    stat_send, stat_recv, near_send, near_recv, cnt_send, cnt_recv, sum_send, sum_recv, all_send, all_recv,
    both_send, both_recv, grad_send, grad_recv, pair_send, pair_recv, out_send, out_recv, local,
):
    vectors, depth = w.shape
    cents = c.shape[0]
    block = vectors // groups
    half = vectors // 2
    piece = half // groups
    share = cents // peers
    chips = peers // CORES
    ring_y = chips // PAIR
    ring_z = groups // PAIR
    rows_of = cents // ring_y
    owners = PAIR * CORES
    step = min(64, rows_of)
    vec = lax.axis_index("vec")
    cent = lax.axis_index("cent")
    chip, core = vec // CORES, lax.rem(vec, CORES)
    y, x_low = chip // PAIR, lax.rem(chip, PAIR)
    x_high, z = cent // ring_z, lax.rem(cent, ring_z)
    sibling = {"vec": vec + 1 - 2 * core}
    scale = 2.0 * depth ** (-0.5)
    slope = 2.0 * depth ** (-0.5) * LOG2E
    offset = depth ** (-0.5) * LOG2E

    def start(src, dst, send, recv, device):
        pltpu.make_async_remote_copy(
            src_ref=src, dst_ref=dst, send_sem=send, recv_sem=recv,
            device_id=device, device_id_type=MESH,
        ).start()

    def wait(ref, sem):
        pltpu.make_async_copy(ref, ref, sem).wait()

    def apart(work):
        pl.when(vec >= 0)(work)

    def cent_at(far):
        return {"cent": lax.rem(cent + far, groups)}

    def chip_at(far):
        return lax.rem(chip + far, chips)

    def cols_of(j):
        return pl.ds(pl.multiple_of(j * block, block), block)

    def chunk_of(t):
        return lax.rem(y + 1 + t, ring_y)

    def rows_at(r):
        return pl.ds(pl.multiple_of(r * rows_of, rows_of), rows_of)

    def chunk(t):
        return slice(t * rows_of, (t + 1) * rows_of)

    def place(t, low, of_core):
        at = t * rows_of + (low * CORES + of_core) * share
        return pl.ds(pl.multiple_of(at, share), share)

    loads = [
        pltpu.make_async_copy(src, dst, local.at[3 + n])
        for n, (src, dst) in enumerate(((w_hbm, w), (g_hbm, g)))
    ]
    for t in range(ring_y):
        pltpu.make_async_copy(c_hbm.at[rows_at(chunk_of(t)), :], c.at[chunk(t), :], local.at[5]).start()
    for load in loads:
        load.start()

    barrier = pltpu.get_barrier_semaphore()
    pl.semaphore_signal(barrier, inc=1, device_id=sibling, device_id_type=MESH)
    for far in range(1, chips):
        there = {"vec": chip_at(far) * CORES + core}
        pl.semaphore_signal(barrier, inc=1, device_id=there, device_id_type=MESH)
    for far in range(1, groups):
        pl.semaphore_signal(barrier, inc=1, device_id=cent_at(far), device_id_type=MESH)

    def expo_block(cols, top, scores, cot):
        total = dots = 0.0
        for at in range(0, cents, step):
            expo = jnp.exp2(scores[at : at + step, cols] - top)
            scores[at : at + step, cols] = expo
            total = total + folded(expo)
            if cot is not None:
                dots = dots + folded(expo * cot[at : at + step, cols])
        total = jnp.sum(total, axis=0, keepdims=True)
        if cot is None:
            return top, total
        return top, total, jnp.sum(dots, axis=0, keepdims=True)

    def keep_stats(which, j, values):
        for line, value in enumerate(values):
            inner = slice(line * block, (line + 1) * block)
            stat_out[which, j, :, inner] = value
            stat_in[which, j, 0, :, inner] = value

    def send_stats(which, j):
        lanes = slice(0, STATS[which] * block)
        for far in range(1, groups):
            start(
                stat_out.at[which, j, :, lanes],
                stat_in.at[which, j, groups - far, :, lanes],
                stat_send.at[which],
                stat_recv.at[which, j],
                cent_at(far),
            )

    def wait_stats(which, j):
        lanes = slice(0, STATS[which] * block)
        wait(stat_in.at[which, j, 1:groups, :, lanes], stat_recv.at[which, j])

    def stat(which, j, q, line):
        return stat_in[which, j, q, :, line * block : (line + 1) * block]

    pltpu.make_async_copy(c, c, local.at[5]).wait()
    for at in range(0, cents, step):
        f = c[at : at + step, :].astype(F32)
        total = jnp.sum(f * f, axis=1, keepdims=True) * offset
        sb[at : at + step, :] = jnp.broadcast_to(total, (step, block))
    loads[0].wait()

    def first_scores(j):
        cols = slice(j * block, (j + 1) * block)
        cross = dot_nt(c[...], w[cols, :])
        top = None
        for at in range(0, cents, step):
            score = cross[at : at + step] * slope - sb[at : at + step, :]
            e1[at : at + step, cols] = score
            here = peaked(score)
            top = here if top is None else jnp.maximum(top, here)
        return jnp.max(top, axis=0, keepdims=True)

    tops = [first_scores(0)]
    for j in range(groups):
        if j + 1 < groups:
            tops.append(first_scores(j + 1))
        keep_stats(0, j, expo_block(slice(j * block, (j + 1) * block), tops[j], e1, None))
    pl.semaphore_wait(barrier, chips + groups - 1)
    for j in range(groups):
        send_stats(0, j)
    ct[...] = c[...].astype(F32).T.astype(BF16)

    def combine(which, j):
        peak = stat(which, j, 0, 0)
        for q in range(1, groups):
            peak = jnp.maximum(peak, stat(which, j, q, 0))
        total = dots = 0.0
        for q in range(groups):
            part_of = jnp.exp2(stat(which, j, q, 0) - peak)
            total = total + part_of * stat(which, j, q, 1)
            if STATS[which] > 2:
                dots = dots + part_of * stat(which, j, q, 2)
        mine = jnp.exp2(stat(which, j, 0, 0) - peak)
        return mine / total, dots / total

    for j in range(groups):
        wait_stats(0, j)
    for j in range(groups):
        row1[j, 0:1, :] = combine(0, j)[0]

    def to_sibling(which, t):
        for q in range(PAIR):
            theirs = q * CORES + 1 - core
            start(
                near_out.at[which, t, theirs],
                near_in.at[which, t, q],
                near_send.at[which],
                near_recv.at[which, t],
                sibling,
            )
        if which == 0:
            start(cnt_out.at[t], cnt_near.at[t], cnt_send.at[0], cnt_recv.at[t], sibling)

    def to_owners(which, t):
        wait(near_in.at[which, t], near_recv.at[which, t])
        if which == 0:
            wait(cnt_near.at[t], cnt_recv.at[t])
            cnt_both[t] = cnt_out[t] + cnt_near[t]
        for d in range(PAIR):
            low = lax.rem(x_low + d, PAIR)
            total = near_out[which, t, low * CORES + core] + near_in[which, t, low]
            if t == ring_y - 1 and d == 0:
                sum_in[which, 0] = total.astype(BF16)
                if which == 0:
                    cnt_in[0] = cnt_both[t]
                continue
            n = t * PAIR + d
            sum_out[which, n] = total.astype(BF16)
            there = chunk_of(t) * PAIR + low
            slot = lax.rem(chip - there + chips, chips)
            device = {"vec": there * CORES + core}
            start(sum_out.at[which, n], sum_in.at[which, slot], sum_send.at[which], sum_recv.at[which], device)
            if which == 0:
                start(cnt_both.at[t], cnt_in.at[slot], cnt_send.at[1], cnt_recv.at[ring_y], device)

    def by_chunks(which, prepare, product):
        for t in range(ring_y):

            @apart
            def _():
                prepare(t)
                value = product(t)
                for q in range(owners):
                    near_out[which, t, q] = value[q * share : (q + 1) * share]

            to_sibling(which, t)
            if t > 1:
                to_owners(which, t - 2)
        for t in range(ring_y - 2, ring_y):
            to_owners(which, t)

    def summed_up(which):
        wait(sum_in.at[which, 1:chips], sum_recv.at[which])
        total = sum_in[which, 0].astype(F32)
        for q in range(1, chips):
            total = total + sum_in[which, q].astype(F32)
        return total

    turns = sorted(range(ring_y), key=lambda d: min(d, ring_y - d))

    def sources(n):
        row = lax.rem(y + turns[n], ring_y)
        for d in range(PAIR):
            low = lax.rem(x_low + d, PAIR)
            there = row * PAIR + low
            yield turns[n] or d, there, low, lax.rem(there - chip + chips, chips)

    def chunk_in(n):
        return (turns[n] - 1) % ring_y

    def to_all(which, own, everywhere):
        for n in range(ring_y):
            at = place((-turns[n] - 1) % ring_y, x_low, core)
            for other_chip, there, _, far in sources(n):
                if other_chip:
                    start(
                        own, everywhere.at[at, :],
                        all_send.at[which], all_recv.at[which, lax.rem(chips - far, chips)],
                        {"vec": there * CORES + core},
                    )
                else:
                    start(own, everywhere.at[at, :], both_send.at[which], both_recv.at[which, 0], sibling)
        everywhere[place(ring_y - 1, x_low, core), :] = own[...]

    def arrive(which, everywhere, n):
        for other_chip, _, low, far in sources(n):
            if other_chip:
                at = place(chunk_in(n), low, core)
                wait(everywhere.at[at, :], all_recv.at[which, far])
                start(
                    everywhere.at[at, :], everywhere.at[at, :],
                    both_send.at[which], both_recv.at[which, far], sibling,
                )

    def gathered(which, everywhere, work):
        def finish(n):
            for _, _, low, far in sources(n):
                at = place(chunk_in(n), low, 1 - core)
                wait(everywhere.at[at, :], both_recv.at[which, far])
            if work is not None:
                apart(lambda: work(chunk_in(n)))

        arrive(which, everywhere, 0)
        finish(0)
        arrive(which, everywhere, 1)
        for n in range(1, ring_y):
            if n + 1 < ring_y:
                arrive(which, everywhere, n + 1)
            finish(n)

    def lane_sums(at, totals):
        for n, total in enumerate(totals):
            here = slice(at + n * step, at + (n + 1) * step)
            column[here, :] = jnp.broadcast_to(jnp.sum(total, axis=1, keepdims=True), (step, LANES))

    def mass_prepare(t):
        counts = [0.0] * (rows_of // step)
        for j in range(groups):
            cols = slice(j * block, (j + 1) * block)
            for n in range(len(counts)):
                here = slice(t * rows_of + n * step, t * rows_of + (n + 1) * step)
                resp = e1[here, cols] * row1[j, 0:1, :]
                r1b[here, cols] = resp.astype(BF16)
                counts[n] = counts[n] + lane_folded(resp)
        lane_sums(t * rows_of, counts)
        cnt_out[t] = column[chunk(t), :].T[0:1, :]

    by_chunks(0, mass_prepare, lambda t: dot_nn(r1b[chunk(t), :], w[...]))

    wait(cnt_in.at[1:chips], cnt_recv.at[ring_y])
    count = cnt_in[0]
    for q in range(1, chips):
        count = count + cnt_in[q]
    column[chunk(0), :] = jnp.broadcast_to(count, (LANES, rows_of)).T
    den[...] = column[place(0, x_low, core), :] + 1e-6
    own_moved[...] = (summed_up(0) / wide(den[...], depth)).astype(BF16)
    to_all(0, own_moved, moved)

    loads[1].wait()
    top_acc[...] = jnp.full_like(top_acc, -jnp.inf)

    def second_rows(t):
        rows = chunk(t)
        own = moved[rows, :]
        f = own.astype(F32)
        square = jnp.sum(f * f, axis=1, keepdims=True) * offset
        for j in range(groups):
            cols = slice(j * block, (j + 1) * block)
            score = dot_nt(own, w[cols, :]) * slope - square
            e2[rows, cols] = score
            top_acc[:, cols] = jnp.maximum(top_acc[:, cols], peaked(score))
            ds[rows, cols] = dot_nt(own, g[cols, :])

    gathered(0, moved, second_rows)

    def second_block(j, carry):
        cols = cols_of(j)
        top = jnp.max(top_acc[:, cols], axis=0, keepdims=True)
        keep_stats(1, j, expo_block(cols, top, e2, ds))
        send_stats(1, j)
        return carry

    lax.fori_loop(0, groups, second_block, 0)
    mt[...] = moved[...].astype(F32).T.astype(BF16)

    for j in range(groups):
        wait_stats(1, j)
    for j in range(groups):
        factor, dots = combine(1, j)
        row2[j, 0:1, :] = factor
        row2[j, 1:2, :] = dots

    def cot_prepare(t):
        totals = [0.0] * (rows_of // step)
        for j in range(groups):
            cols = slice(j * block, (j + 1) * block)
            for n in range(len(totals)):
                here = slice(t * rows_of + n * step, t * rows_of + (n + 1) * step)
                second = e2[here, cols] * row2[j, 0:1, :]
                r2b[here, cols] = second.astype(BF16)
                edge = second * (ds[here, cols] - row2[j, 1:2, :]) * scale
                eb[here, cols] = edge.astype(BF16)
                totals[n] = totals[n] + lane_folded(edge)
        lane_sums(t * rows_of, totals)

    def cot_product(t):
        rows = chunk(t)
        cot = dot_nn(r2b[rows, :], g[...]) + dot_nn(eb[rows, :], w[...])
        return cot - wide(column[rows, :], depth) * moved[rows, :].astype(F32)

    by_chunks(1, cot_prepare, cot_product)

    def part_block(j, carry):
        cols = pl.ds(pl.multiple_of(j * 2 * block, 2 * block), 2 * block)
        part[:, cols] = dot_nn(mt[...], eb[:, cols])
        return carry

    lax.fori_loop(0, groups // 2, part_block, 0)

    own_mean[...] = (summed_up(1) / wide(den[...], depth)).astype(BF16)
    to_all(1, own_mean, mean)

    top_acc[...] = jnp.zeros_like(top_acc)

    def third_rows(t):
        rows = chunk(t)
        own = mean[rows, :]
        shift = jnp.sum(own.astype(F32) * moved[rows, :].astype(F32), axis=1, keepdims=True)
        for j in range(groups):
            cols = slice(j * block, (j + 1) * block)
            dfirst = dot_nt(own, w[cols, :]) - shift
            ds[rows, cols] = dfirst
            top_acc[:, cols] += folded(e1[rows, cols] * dfirst)

    gathered(1, mean, third_rows)
    for j in range(groups):
        cols = slice(j * block, (j + 1) * block)
        keep_stats(2, j, (jnp.sum(top_acc[:, cols], axis=0, keepdims=True) * row1[j, 0:1, :],))
        send_stats(2, j)
    mt[...] = mean[...].astype(F32).T.astype(BF16)

    def mean_block(j, carry):
        cols = pl.ds(pl.multiple_of(j * 2 * block, 2 * block), 2 * block)
        part[:, cols] += dot_nn(mt[...], r1b[:, cols])
        return carry

    lax.fori_loop(0, groups // 2, mean_block, 0)

    in_half = groups // 2

    def block_at(u):
        h, t = u // in_half, lax.rem(u, in_half)
        far_x = lax.rem(t, PAIR)
        two_z = lax.rem(z // 2 + 1 + t // PAIR, ring_z // 2)
        return h, h * in_half + far_x * (ring_z // 2) + two_z, far_x, two_z * 2

    def grad_block(u, carry):
        h, j, to_x, first_z = block_at(u)
        cols = cols_of(j)
        wait_stats(2, j)
        dots = stat(2, j, 0, 0)
        for q in range(1, groups):
            dots = dots + stat(2, j, q, 0)
        factor = row1[j, 0:1, :]
        for at in range(0, cents, step):
            first = e1[at : at + step, cols] * factor
            edge = first * (ds[at : at + step, cols] - dots) * scale
            eb[at : at + step, cols] = edge.astype(BF16)
            total = lane_folded(edge)

            @pl.when(u == 0)
            def _():
                esum[at : at + step, :] = total

            @pl.when(u != 0)
            def _():
                esum[at : at + step, :] += total

        grad = part[:, cols] + dot_nn(ct[...], eb[:, cols])
        grad = grad.astype(BF16)
        for q in range(2):
            to_z = first_z + q
            far = lax.rem(to_z - z + ring_z, ring_z)
            slot = lax.rem(ring_z - far, ring_z)
            mine = grad[:, q * piece : (q + 1) * piece]
            grad_out[h, to_x, to_z] = mine

            @pl.when(far != 0)
            def _():
                start(
                    grad_out.at[h, to_x, to_z], grad_in.at[h, slot, to_x],
                    grad_send, grad_recv.at[h], {"cent": x_high * ring_z + to_z},
                )

            @pl.when(far == 0)
            def _():
                grad_in[h, 0, to_x] = mine

        return carry

    lax.fori_loop(0, groups, grad_block, 0)

    other = {"cent": (1 - x_high) * ring_z + z}

    part_d = depth // 2

    def over_z(h, n):
        if n == 0:
            wait(grad_in.at[h, 1:ring_z], grad_recv.at[h])
        for to_x in range(PAIR):
            inner = slice(n * part_d, (n + 1) * part_d)
            total = grad_in[h, 0, to_x, inner, :].astype(F32)
            for q in range(1, ring_z):
                total = total + grad_in[h, q, to_x, inner, :].astype(F32)
            pair_out[h, n, to_x] = total.astype(BF16)
        start(pair_out.at[h, n], pair_in.at[h, n], pair_send, pair_recv.at[h, n], other)

    def grad_place(h, n, to_x):
        rows = h * half + (to_x * ring_z + z) * piece
        return gw.at[pl.ds(pl.multiple_of(rows, piece), piece), n * part_d : (n + 1) * part_d]

    def over_x(h, n):
        wait(pair_in.at[h, n], pair_recv.at[h, n])
        for to_x in range(PAIR):
            total = pair_out[h, n, to_x].astype(F32) + pair_in[h, n, to_x].astype(F32)
            own_grad[h, n, to_x] = total.T.astype(BF16)
        for to_x in range(PAIR):
            place = grad_place(h, n, to_x)
            for far in range(1, ring_z):
                there = {"cent": x_high * ring_z + lax.rem(z + far, ring_z)}
                start(own_grad.at[h, n, to_x], place, out_send, out_recv, there)
            pltpu.make_async_copy(own_grad.at[h, n, to_x], place, local.at[h]).start()

    def start_product(t):
        rows = chunk(t)
        total = jnp.sum(esum[rows, :], axis=1, keepdims=True)
        return dot_nn(eb[rows, :], w[...]) - total * c[rows, :].astype(F32)

    over_z(0, 0)
    over_z(0, 1)
    by_chunks(2, lambda t: None, start_product)
    over_x(0, 0)
    over_x(0, 1)
    over_z(1, 0)
    over_z(1, 1)
    own_start[...] = summed_up(2).astype(BF16)
    to_all(2, own_start, start_all)
    over_x(1, 0)
    over_x(1, 1)
    gathered(2, start_all, None)
    for t in range(ring_y):
        rows = rows_at(chunk_of(t))
        pltpu.make_async_copy(start_all.at[chunk(t), :], gc.at[rows, :], local.at[2]).start()
    wait(gw.at[0 : (ring_z - 1) * 2 * PAIR * piece, :], out_recv)
    for h in range(2):
        wait(gw.at[0 : PAIR * piece, :], local.at[h])
    wait(start_all, local.at[2])

    for which in range(3):
        lanes = slice(0, STATS[which] * block)
        wait(stat_in.at[which, :, 1:groups, :, lanes], stat_send.at[which])
        wait(near_in.at[which], near_send.at[which])
        wait(sum_in.at[which, 1:chips], sum_send.at[which])
        wait(start_all.at[0 : (chips - 1) * share, :], all_send.at[which])
        wait(start_all.at[0 : chips * share, :], both_send.at[which])
    wait(cnt_near, cnt_send.at[0])
    wait(cnt_in.at[1:chips], cnt_send.at[1])
    wait(grad_in.at[:, 1:ring_z], grad_send)
    wait(pair_in, pair_send)
    wait(gw.at[0 : (ring_z - 1) * 2 * PAIR * piece, :], out_send)


def body(peers, groups, weights, centroids, cotangent):
    vectors, depth = weights.shape
    cents = centroids.shape[0]
    block = vectors // groups
    piece = vectors // 2 // groups
    share = cents // peers
    chips = peers // CORES
    ring_y = chips // PAIR
    ring_z = groups // PAIR
    rows_of = cents // ring_y
    owners = PAIR * CORES
    vmem = pltpu.VMEM
    dma = pltpu.SemaphoreType.DMA
    scratch = [
        vmem((vectors, depth), BF16),
        vmem((cents, depth), BF16),
        vmem((vectors, depth), BF16),
        vmem((8, vectors), F32),
        vmem((cents, vectors), F32),
        vmem((cents, vectors), F32),
        vmem((cents, vectors), F32),
        vmem((cents, vectors), BF16),
        vmem((cents, vectors), BF16),
        vmem((cents, vectors), BF16),
        vmem((cents, block), F32),
        vmem((depth, cents), BF16),
        vmem((depth, cents), BF16),
        vmem((cents, depth), BF16),
        vmem((cents, depth), BF16),
        vmem((depth, vectors), F32),
        vmem((cents, LANES), F32),
        vmem((cents, LANES), F32),
        vmem((share, LANES), F32),
        vmem((3, groups, 1, 3 * block), F32),
        vmem((3, groups, groups, 1, 3 * block), F32),
        vmem((groups, 8, block), F32),
        vmem((groups, 8, block), F32),
        vmem((ring_y, 1, rows_of), F32),
        vmem((ring_y, 1, rows_of), F32),
        vmem((ring_y, 1, rows_of), F32),
        vmem((chips, 1, rows_of), F32),
        vmem((3, ring_y, owners, share, depth), F32),
        vmem((3, ring_y, PAIR, share, depth), F32),
        vmem((3, chips, share, depth), BF16),
        vmem((3, chips, share, depth), BF16),
        vmem((share, depth), BF16),
        vmem((share, depth), BF16),
        vmem((share, depth), BF16),
        vmem((cents, depth), BF16),
        vmem((2, PAIR, ring_z, depth, piece), BF16),
        vmem((2, ring_z, PAIR, depth, piece), BF16),
        vmem((2, 2, PAIR, depth // 2, piece), BF16),
        vmem((2, 2, PAIR, depth // 2, piece), BF16),
        vmem((2, 2, PAIR, piece, depth // 2), BF16),
        dma((3,)),
        dma((3, groups)),
        dma((3,)),
        dma((3, ring_y)),
        dma((2,)),
        dma((ring_y + 1,)),
        dma((3,)),
        dma((3,)),
        dma((3,)),
        dma((3, chips)),
        dma((3,)),
        dma((3, chips)),
        dma,
        dma((2,)),
        dma,
        dma((2, 2)),
        dma,
        dma,
        dma((6,)),
    ]
    grad_rows, start_cot = pl.pallas_call(
        functools.partial(kernel, peers, groups),
        out_shape=(
            jax.ShapeDtypeStruct((vectors, depth), BF16),
            jax.ShapeDtypeStruct((cents, depth), BF16),
        ),
        in_specs=[pl.BlockSpec(memory_space=pl.ANY)] * 3,
        out_specs=[pl.BlockSpec(memory_space=pl.ANY)] * 2,
        scratch_shapes=scratch,
        compiler_params=pltpu.CompilerParams(
            collective_id=0, has_side_effects=True, vmem_limit_bytes=67043328
        ),
        name="soft_assignments",
    )(weights, centroids, cotangent)
    return grad_rows, start_cot.astype(F32)


def solution(mesh):
    return jax.shard_map(
        functools.partial(body, mesh.shape["vec"], mesh.shape["cent"]),
        mesh=mesh,
        in_specs=(P("vec", None), P("cent", None), P("vec", None)),
        out_specs=(P("vec", None), P("cent", None)),
        check_vma=False,
    )
```
